256 devices in a mesh: cell: 32 (over z_hi, x, core), mode: 8 (over z_lo, y).
Axes of the slice: x: 4, y: 4, z: 8 (z_hi: 4, z_lo: 2; z = z_hi * 2 + z_lo), core: 2. Of those that a mesh axis runs over, the one named last changes fastest.
Arguments:
- pod_modes: bfloat16 [3, 512, 4, 64, 128], P(None, 'mode', None, 'cell'), may hold values from -6 to 6
- slab_map: int32 [4, 64, 128], P(None, 'cell'), may hold values from 0 to 7
- slab_volume: float32 [8], replicated, may hold values from 0.25 to 4
- advect_index: int32 [8], replicated, may hold values from 0 to 511, as said below
- pair_adv: int32 [2048], replicated, may hold values from 0 to 7
- pair_mode: int32 [2048], replicated, may hold values from 0 to 511
- pair_amp: float32 [2048, 1024], replicated, may hold values from -0.2 to 0.2
Outputs:
- convective: float32 [512, 8, 512], P(('mode', 'cell'))
- response: float32 [512, 1024], P(('mode', 'cell'))
The draws below stay inside these ranges and needn't reach their ends.
Inputs may be any that keep to these rules, and one draw needn't show every extreme that they name: `advect_index`: 8 distinct mode indices.
All inputs are finite; a program needn't handle non-finite values.
Results may differ from the reference program's by a relative error of at most 0.0043.
Values may be sent and summed in bfloat16 or wider, within the bound.
A program may use at most 128 MiB of HBM per device.

```python
import math
import jax
import jax.numpy as jnp
from jax import lax

M = 512
J = 8
P_SIZE = 2048
S = 1024
SLABS = 8
NX = 4
NZ = 128
NY = 64


def draw_advect_index(key, part):
    return jax.random.permutation(key, M)[:J].astype(jnp.int32)


def with_ends(result, own_key, low, top_value):
    extent = result.shape
    spot = [jax.random.randint(jax.random.fold_in(own_key, axis), (), 0, extent[axis]) for axis in range(len(extent))]
    result = result.at[tuple(spot)].set(low)
    longest = extent.index(max(extent))
    spot[longest] = (spot[longest] + 1) % extent[longest]
    return result.at[tuple(spot)].set(top_value)


def levels(own_key, dims, cuts, low, top_value):
    def one(axis_at, shards_of):
        draws = jax.random.uniform(jax.random.fold_in(jax.random.fold_in(own_key, 6), axis_at), (shards_of,), jnp.float32, low / len(cuts), top_value / len(cuts))
        return jnp.repeat(jnp.exp(draws), dims[axis_at] // shards_of).reshape((-1,) + (1,) * (len(dims) - axis_at - 1))

    gain = one(*cuts[0])
    for cut in cuts[1:]:
        gain = gain * one(*cut)
    return gain


def normal_values(stream_key, extent, scale, reach, pieces=(), kind=jnp.bfloat16):
    result = jax.random.normal(stream_key, extent, jnp.float32) * scale
    if len(pieces) > 0:
        result = levels(stream_key, extent, pieces, -0.22, 0.18) * result
    return jnp.clip(result, min=-reach, max=reach).astype(kind)


def setup_inputs(seed: int = 0) -> dict:
    key_list = jax.random.split(jax.random.key(seed), 8)
    pod_modes = normal_values(key_list[0], (3, M, NX, NY, NZ), 1.0, 6.0, ((1, 8), (3, 32)))
    slab_map = with_ends(jax.random.randint(key_list[1], (NX, NY, NZ), 0, SLABS), jax.random.fold_in(key_list[1], 1), 0, SLABS - 1).astype(jnp.int32)
    slab_volume = jnp.clip(jnp.exp(jax.random.uniform(key_list[2], (SLABS,), jnp.float32, math.log(0.25), math.log(4.0))), 0.25, 4.0)
    advect_index = draw_advect_index(jax.random.fold_in(key_list[7], 71), 0)
    pair_adv = with_ends(jax.random.randint(key_list[4], (P_SIZE,), 0, J), jax.random.fold_in(key_list[4], 1), 0, J - 1).astype(jnp.int32)
    pair_mode = with_ends(jax.random.randint(key_list[5], (P_SIZE,), 0, M), jax.random.fold_in(key_list[5], 1), 0, M - 1).astype(jnp.int32)
    pair_amp = normal_values(key_list[6], (P_SIZE, S), 0.03, 0.2, (), jnp.float32)
    return {"pod_modes": pod_modes, "slab_map": slab_map, "slab_volume": slab_volume, "advect_index": advect_index, "pair_adv": pair_adv, "pair_mode": pair_mode, "pair_amp": pair_amp}


def grads_of(field):
    along_x = 0.5 * (jnp.roll(field, -1, axis=2) - jnp.roll(field, 1, axis=2))
    padded = jnp.pad(field, ((0, 0), (0, 0), (0, 0), (1, 1), (0, 0)))
    along_y = 0.5 * (padded[:, :, :, 2:] - padded[:, :, :, :-2])
    along_z = 0.5 * (jnp.roll(field, -1, axis=4) - jnp.roll(field, 1, axis=4))
    return jnp.stack([along_x, along_y, along_z])


def reference(pod_modes, slab_map, slab_volume, advect_index, pair_adv, pair_mode, pair_amp):
    cell_total = NX * NY * NZ
    field = pod_modes.astype(jnp.float32)
    rounded = lax.optimization_barrier(grads_of(field).astype(jnp.bfloat16))
    grads = rounded.astype(jnp.float32).reshape(3, 3, M, cell_total)
    volume = slab_volume[slab_map].reshape(cell_total)
    flat_modes = pod_modes.astype(jnp.float32).reshape(3, M, cell_total)
    weighted = flat_modes[:, advect_index] * volume
    rows_per = 8

    def one_block(start_at):
        rows = lax.dynamic_slice_in_dim(flat_modes, start_at, rows_per, 1)
        left_factor = rows.transpose(1, 0, 2)[:, None, None, :, :] * weighted.transpose(1, 0, 2)[None, :, :, None, :]
        left_factor = lax.optimization_barrier(left_factor.astype(jnp.bfloat16)).astype(jnp.float32)
        return jnp.einsum("ijdcx,dckx->ijk", left_factor, grads)

    starts = (jnp.arange(M // rows_per) * rows_per).astype(jnp.int32)
    convective = lax.map(one_block, starts).reshape(M, J, M) * (cell_total ** -0.5)
    flat_rows = convective.reshape(M, J * M)
    pair_slot = pair_adv * M + pair_mode
    columns = jnp.take(flat_rows, pair_slot, axis=1)
    response = jnp.dot(columns, pair_amp, precision=lax.Precision.HIGHEST, preferred_element_type=jnp.float32)
    return convective, response
```

```python
import functools
import jax
import jax.numpy as jnp
from jax import lax
from jax.experimental import pallas as pl
from jax.experimental.pallas import tpu as pltpu
from jax.sharding import PartitionSpec as P

MESH = pl.DeviceIdType.MESH
F32 = jnp.float32
BF16 = jnp.bfloat16
NT = (((1,), (1,)), ((), ()))


def kernel(
    scale,
    u_ref, slab_ref, vol_ref, adv_ref, padv_ref, pmode_ref, amp_hbm,
    out_ref, resp_ref,
    blk, hal, up, um, q_ref,
    part, rs_buf, h_ref, hyh, hzp, hzm, v_ref,
    tf, tb, xbuf, zsrc, zbuf, fin,
    amp, amp_hi, amp_lo, onehot, mask,
    rs_s, rs_r, ag_s, ag_r, bulk_s, bulk_r, halo_s, halo_r, hy_s, hy_r, x_s, x_r, z_s, z_r, amp_sem,
):
    q = lax.axis_index("cell")
    m = lax.axis_index("mode")
    e = lax.rem(q, 8)
    zh = q // 8
    z = m // 4
    y = lax.rem(m, 4)
    ynext = lax.rem(y + 1, 4)
    yprev = lax.rem(y + 3, 4)
    yfar = lax.rem(y + 2, 4)
    qprev = lax.rem(q + 31, 32)
    qnext = lax.rem(q + 1, 32)

    def dev(cell, mode):
        return {"cell": cell, "mode": mode}

    def rcopy(src, dst, send, recv, target):
        return pltpu.make_async_remote_copy(
            src_ref=src, dst_ref=dst, send_sem=send, recv_sem=recv,
            device_id=target, device_id_type=MESH,
        )

    here = dev(q, m)
    m_ring = [lax.rem(m + t, 8) for t in range(8)]
    e_ring = [zh * 8 + lax.rem(e + t, 8) for t in range(8)]
    z_ring = [lax.rem(zh + t, 4) * 8 + e for t in range(4)]

    barrier = pltpu.get_barrier_semaphore()
    peers = [dev(q, m_ring[t]) for t in range(1, 8)]
    peers += [dev(e_ring[t], m) for t in range(1, 8)]
    peers += [dev(z_ring[t], m) for t in range(1, 4)]
    peers += [dev(qprev, m), dev(qnext, m)]
    for peer in peers:
        pl.semaphore_signal(barrier, inc=1, device_id=peer, device_id_type=MESH)
    amp_copy = pltpu.make_async_copy(amp_hbm, amp, amp_sem)
    amp_copy.start()

    sub = lax.broadcasted_iota(jnp.int32, (8, 64), 0)
    wanted = jnp.zeros((8, 64), jnp.int32)
    for j in range(8):
        wanted = jnp.where(sub == j, adv_ref[j], wanted)
    owned = (wanted == m * 64 + lax.broadcasted_iota(jnp.int32, (8, 64), 1)).astype(F32).astype(BF16)
    for row in range(2):
        picked = jnp.dot(owned, u_ref[row], preferred_element_type=F32)
        for d in range(3):
            for x in range(4):
                at = (d * 4 + x) * 128
                part[row * 4 + x, d] = picked[:, at : at + 128]
    pl.semaphore_wait(barrier, len(peers))

    rs = [None]
    for t in range(1, 8):
        copy = rcopy(part.at[m_ring[t]], rs_buf.at[t], rs_s.at[t], rs_r.at[t], dev(q, m_ring[t]))
        copy.start()
        rs.append(copy)

    up_y = dev(q, z * 4 + ynext)
    down_y = dev(q, z * 4 + yprev)
    to_z = dev(q, (1 - z) * 4 + y)

    def piece(ref, p):
        return ref.at[p // 2, pl.ds((p % 2) * 32, 32)]

    def move(src, slot, p, target):
        return rcopy(piece(src, p), piece(blk.at[slot], p), bulk_s.at[slot * 4 + p], bulk_r.at[slot * 4 + p], target)

    started = []

    def go(src, slot, p, target):
        copy = move(src, slot, p, target)
        copy.start()
        started.append(copy)

    def arrived(slot, p):
        move(u_ref, slot, p, here).wait_recv()

    def start_own(p):
        go(u_ref, 0, p, up_y)
        go(u_ref, 1, p, down_y)
        go(u_ref, 2, p, to_z)

    halo = [
        rcopy(u_ref.at[0], hal.at[1], halo_s.at[0], halo_r.at[0], dev(qprev, m)),
        rcopy(u_ref.at[1], hal.at[0], halo_s.at[1], halo_r.at[1], dev(qnext, m)),
    ]
    start_own(0)
    start_own(1)
    halo[0].start()
    halo[1].start()

    for x in range(4):
        for row in range(2):
            ids = slab_ref[x, row : row + 1, :]
            vol = jnp.zeros((1, 128), F32)
            for level in range(8):
                vol = jnp.where(ids == level, vol_ref[level], vol)
            v_ref[row * 4 + x : row * 4 + x + 1, :] = vol * (0.5 * scale)

    def shift(k, carry):
        at = pl.ds(pl.multiple_of(k * 128, 128), 128)
        for row in range(2):
            tile = u_ref[row, :, at].astype(F32)
            up[row, :, at] = pltpu.roll(tile, 127, 1).astype(BF16)
            um[row, :, at] = pltpu.roll(tile, 1, 1).astype(BF16)
        return carry

    lax.fori_loop(0, 12, shift, 0)

    total = part[m]
    for t in range(1, 8):
        rs[t].wait_recv()
        total = total + rs_buf[t]
    h_ref[m] = total * v_ref[pl.ds(m, 1), :][None]
    ag = [None]
    for t in range(1, 8):
        copy = rcopy(h_ref.at[m], h_ref.at[m], ag_s.at[t], ag_r.at[t], dev(q, m_ring[t]))
        copy.start()
        ag.append(copy)
    start_own(2)
    start_own(3)

    def pick_modes(k, carry):
        at = pl.ds(pl.multiple_of(k * 256, 256), 256)
        rows = lax.broadcasted_iota(jnp.int32, (512, 256), 0)
        onehot[:, at] = (rows == pmode_ref[:, at]).astype(F32).astype(BF16)
        return carry

    lax.fori_loop(0, 8, pick_modes, 0)
    mask[...] = (lax.broadcasted_iota(jnp.int32, (8, 2048), 0) == padv_ref[...]).astype(F32)

    for t in range(1, 8):
        ag[t].wait_recv()
    hy = [
        rcopy(h_ref.at[pl.ds(0, 4), 1], hyh.at[1], hy_s.at[0], hy_r.at[0], dev(qprev, m)),
        rcopy(h_ref.at[pl.ds(4, 4), 1], hyh.at[0], hy_s.at[1], hy_r.at[1], dev(qnext, m)),
    ]
    hy[0].start()
    hy[1].start()
    for n in range(8):
        hzp[n] = pltpu.roll(h_ref[n, 2], 127, 1)
        hzm[n] = pltpu.roll(h_ref[n, 2], 1, 1)

    def relay_z(p):
        arrived(2, p)
        go(blk.at[2], 3, p, up_y)
        go(blk.at[2], 4, p, down_y)

    for p in (0, 1):
        arrived(0, p)
        go(blk.at[0], 5, p, up_y)
        relay_z(p)
    for p in (2, 3):
        arrived(1, p)
        go(blk.at[1], 5, p, down_y)
        relay_z(p)

    halo[0].wait_recv()
    halo[1].wait_recv()
    hy[0].wait_recv()
    hy[1].wait_recv()

    first_ok = jnp.where(q == 0, 0.0, 1.0)
    last_ok = jnp.where(q == 31, 0.0, 1.0)

    def build(row, c, carry_in):
        def one(x, carry):
            xp = lax.rem(x + 1, 4)
            xm = lax.rem(x + 3, 4)
            at = pl.ds(pl.multiple_of((c * 4 + x) * 128, 128), 128)
            atp = pl.ds(pl.multiple_of((c * 4 + xp) * 128, 128), 128)
            atm = pl.ds(pl.multiple_of((c * 4 + xm) * 128, 128), 128)
            n = row * 4 + x
            for g in range(2):
                cut = pl.ds(g * 32, 32)
                uxp = u_ref[row, cut, atp].astype(F32)
                uxm = u_ref[row, cut, atm].astype(F32)
                uzp = up[row, cut, at].astype(F32)
                uzm = um[row, cut, at].astype(F32)
                if row == 0:
                    uyp = u_ref[1, cut, at].astype(F32)
                    uym = hal[0, cut, at].astype(F32) * first_ok
                else:
                    uyp = hal[1, cut, at].astype(F32) * last_ok
                    uym = u_ref[0, cut, at].astype(F32)
                for j in range(8):
                    js = slice(j, j + 1)
                    hyp = h_ref[4 + x, 1, js] if row == 0 else hyh[1, x, js]
                    hym = hyh[0, x, js] if row == 0 else h_ref[x, 1, js]
                    qq = h_ref[row * 4 + xm, 0, js] * uxm - h_ref[row * 4 + xp, 0, js] * uxp
                    qq = qq + (hym * uym - hyp * uyp)
                    qq = qq + (hzm[n, js] * uzm - hzp[n, js] * uzp)
                    lines = pl.ds(j * 64 + g * 32, 32)
                    q_ref[row, lines, at] = qq.astype(BF16)
            return carry

        return lax.fori_loop(0, 4, one, carry_in)

    for row in range(2):
        lax.fori_loop(0, 3, functools.partial(build, row), 0)
        for p in (2 * row, 2 * row + 1):
            arrived(5, p)
            go(blk.at[5], 6, p, to_z)

    def send_batch(n):
        tb[n] = tf[...].astype(BF16).reshape(4, 8, 16, 128)
        for t in range(1, 8):
            x_copy(n, t).start()

    def x_copy(n, t):
        return rcopy(
            tb.at[n, :, lax.rem(e + t, 8)], xbuf.at[n, t], x_s.at[n, t], x_r.at[n, t], dev(e_ring[t], m)
        )

    def products(n, low, high):
        total = None
        for r in range(2):
            pair = jnp.concatenate([low[r], high[r]], axis=0)
            value = lax.dot_general(q_ref[r], pair, NT, preferred_element_type=F32)
            total = value if total is None else total + value
        for j in range(8):
            tf[pl.ds(j, 64, stride=8), :] = total[j * 64 : (j + 1) * 64]
        send_batch(n)

    def z_copy(n, t):
        return rcopy(zsrc.at[n, lax.rem(zh + t, 4)], zbuf.at[n, t], z_s.at[n, t], z_r.at[n, t], dev(z_ring[t], m))

    def gather_batch(n):
        total = tb[n, :, e].astype(F32)
        for t in range(1, 8):
            x_copy(n, t).wait_recv()
            total = total + xbuf[n, t].astype(F32)
        zsrc[n] = total
        for t in range(1, 4):
            z_copy(n, t).start()

    products(0, u_ref, blk.at[2])
    for p in range(2):
        arrived(0, 2 + p)
        arrived(1, p)
    products(1, blk.at[0], blk.at[1])
    gather_batch(0)

    amp_copy.wait()

    def split_amp(k, carry):
        at = pl.ds(pl.multiple_of(k * 32, 32), 32)
        value = amp[at]
        hi = value.astype(BF16)
        amp_hi[at] = hi
        amp_lo[at] = (value - hi.astype(F32)).astype(BF16)
        return carry

    lax.fori_loop(0, 64, split_amp, 0)
    gather_batch(1)
    for p in range(4):
        arrived(3, p)
        arrived(4, p)
    products(2, blk.at[3], blk.at[4])
    gather_batch(2)
    for p in range(4):
        arrived(6, p)
    products(3, blk.at[5], blk.at[6])
    gather_batch(3)

    blocks = [
        (m, (1 - z) * 4 + y),
        (z * 4 + yprev, z * 4 + ynext),
        ((1 - z) * 4 + yprev, (1 - z) * 4 + ynext),
        (z * 4 + yfar, (1 - z) * 4 + yfar),
    ]
    for n in range(4):
        value = zsrc[n, zh]
        for t in range(1, 4):
            z_copy(n, t).wait_recv()
            value = value + zbuf[n, t]
        fin[blocks[n][0]] = value
        fin[blocks[n][1]] = pltpu.roll(value, 64, 1)

    low = lax.broadcasted_iota(jnp.int32, (16, 128), 1) < 64
    columns = []
    for t in range(4):
        columns.append(jnp.where(low, fin[2 * t], pltpu.roll(fin[2 * t + 1], 64, 1)))
    tensor = jnp.concatenate(columns, axis=1)
    out_ref[...] = tensor
    top = tensor.astype(BF16)
    rest = (tensor - top.astype(F32)).astype(BF16)
    chosen = jnp.dot(jnp.concatenate([top, rest], axis=0), onehot[...], preferred_element_type=F32)
    chosen = chosen[:16] + chosen[16:]
    first = jnp.sum(chosen[:8] * mask[...], axis=0, keepdims=True)
    second = jnp.sum(chosen[8:] * mask[...], axis=0, keepdims=True)
    rows = lax.broadcasted_iota(jnp.int32, (16, 2048), 0)
    both = jnp.where(lax.rem(rows, 2) == 0, first, second)
    both_hi = both.astype(BF16).astype(F32)
    stacked = jnp.where(rows < 2, both_hi, jnp.where(rows < 4, both - both_hi, 0.0)).astype(BF16)
    answer = jnp.dot(stacked, amp_hi[...], preferred_element_type=F32)
    answer = answer + jnp.dot(stacked, amp_lo[...], preferred_element_type=F32)
    resp_ref[...] = answer[0:2] + answer[2:4]

    for t in range(1, 8):
        rs[t].wait_send()
        ag[t].wait_send()
    for copy in started + halo + hy:
        copy.wait_send()
    for n in range(4):
        for t in range(1, 8):
            x_copy(n, t).wait_send()
        for t in range(1, 4):
            z_copy(n, t).wait_send()


def shards(pod_modes, slab_map, slab_volume, advect_index, pair_adv, pair_mode, pair_amp):
    cells = pod_modes.shape[2] * pod_modes.shape[3] * lax.axis_size("cell") * pod_modes.shape[4]
    u = jnp.transpose(pod_modes, (3, 1, 0, 2, 4)).reshape(2, 64, 1536)
    vmem = pl.BlockSpec(memory_space=pltpu.VMEM)
    smem = pl.BlockSpec(memory_space=pltpu.SMEM)
    dma = pltpu.SemaphoreType.DMA
    tensor, response = pl.pallas_call(
        functools.partial(kernel, float(cells) ** -0.5),
        out_shape=(
            jax.ShapeDtypeStruct((16, 512), F32),
            jax.ShapeDtypeStruct((2, 1024), F32),
        ),
        in_specs=[vmem, vmem, smem, smem, vmem, vmem, pl.BlockSpec(memory_space=pl.ANY)],
        out_specs=(vmem, vmem),
        scratch_shapes=[
            pltpu.VMEM((7, 2, 64, 1536), BF16),
            pltpu.VMEM((2, 64, 1536), BF16),
            pltpu.VMEM((2, 64, 1536), BF16),
            pltpu.VMEM((2, 64, 1536), BF16),
            pltpu.VMEM((2, 512, 1536), BF16),
            pltpu.VMEM((8, 3, 8, 128), F32),
            pltpu.VMEM((8, 3, 8, 128), F32),
            pltpu.VMEM((8, 3, 8, 128), F32),
            pltpu.VMEM((2, 4, 8, 128), F32),
            pltpu.VMEM((8, 8, 128), F32),
            pltpu.VMEM((8, 8, 128), F32),
            pltpu.VMEM((8, 128), F32),
            pltpu.VMEM((512, 128), F32),
            pltpu.VMEM((4, 4, 8, 16, 128), BF16),
            pltpu.VMEM((4, 8, 4, 16, 128), BF16),
            pltpu.VMEM((4, 4, 16, 128), F32),
            pltpu.VMEM((4, 4, 16, 128), F32),
            pltpu.VMEM((8, 16, 128), F32),
            pltpu.VMEM((2048, 1024), F32),
            pltpu.VMEM((2048, 1024), BF16),
            pltpu.VMEM((2048, 1024), BF16),
            pltpu.VMEM((512, 2048), BF16),
            pltpu.VMEM((8, 2048), F32),
            dma((8,)), dma((8,)), dma((8,)), dma((8,)),
            dma((28,)), dma((28,)), dma((2,)), dma((2,)), dma((2,)), dma((2,)),
            dma((4, 8)), dma((4, 8)), dma((4, 4)), dma((4, 4)), dma,
        ],
        compiler_params=pltpu.CompilerParams(
            collective_id=0, has_side_effects=True, vmem_limit_bytes=60 * 2**20
        ),
        name="pod_tensor",
    )(
        u, slab_map, slab_volume, advect_index,
        pair_adv.reshape(1, -1), pair_mode.reshape(1, -1), pair_amp,
    )
    return tensor.reshape(2, 8, 512), response


def solution(mesh):
    in_specs = (P(None, "mode", None, "cell", None), P(None, "cell", None), P(), P(), P(), P(), P())
    out_specs = (P(("mode", "cell"), None, None), P(("mode", "cell"), None))
    return jax.shard_map(shards, mesh=mesh, in_specs=in_specs, out_specs=out_specs, check_vma=False)
```

```python
import functools
import jax
import jax.numpy as jnp
from jax import lax
from jax.experimental import pallas as pl
from jax.experimental.pallas import tpu as pltpu
from jax.sharding import PartitionSpec as P

MESH = pl.DeviceIdType.MESH
F32 = jnp.float32
BF16 = jnp.bfloat16
NT = (((1,), (1,)), ((), ()))


def kernel(
    scale,
    u_ref, slab_ref, vol_ref, adv_ref, padv_ref, pmode_ref, amp_hbm,
    out_ref, resp_ref,
    ub, blk, hal, up, um, q_ref,
    part, rs_buf, h_ref, hyh, hzp, hzm,
    tf, tb, xbuf, zsrc, zbuf, fin,
    amp, amp_hi, amp_lo, onehot, mask,
    rs_s, rs_r, ag_s, ag_r, own_s, own_r, bulk_s, bulk_r, halo_s, halo_r, hy_s, hy_r, x_s, x_r, z_s, z_r, amp_sem,
):
    q = lax.axis_index("cell")
    m = lax.axis_index("mode")
    core = lax.rem(q, 2)
    e = lax.rem(q, 8)
    zh = q // 8
    z = m // 4
    y = lax.rem(m, 4)
    stays = core == z
    vq = q - core + z
    vm = core * 4 + y
    ynext = lax.rem(y + 1, 4)
    yprev = lax.rem(y + 3, 4)
    yfar = lax.rem(y + 2, 4)

    def place(cell, block):
        return dev(cell - lax.rem(cell, 2) + block // 4, lax.rem(cell, 2) * 4 + lax.rem(block, 4))

    def dev(cell, mode):
        return {"cell": cell, "mode": mode}

    def rcopy(src, dst, send, recv, target):
        return pltpu.make_async_remote_copy(
            src_ref=src, dst_ref=dst, send_sem=send, recv_sem=recv,
            device_id=target, device_id_type=MESH,
        )

    here = dev(q, m)
    n_ring = [lax.rem(vm + t, 8) for t in range(8)]
    e_ring = [lax.rem(e + t, 8) for t in range(8)]
    z_ring = [lax.rem(zh + t, 4) * 8 + e for t in range(4)]
    vprev = lax.rem(vq + 31, 32)
    vnext = lax.rem(vq + 1, 32)
    qprev = lax.rem(q + 31, 32)
    qnext = lax.rem(q + 1, 32)

    barrier = pltpu.get_barrier_semaphore()
    y_of = [lax.rem(y + t, 4) for t in range(4)]
    peers = [place(vq, n_ring[t]) for t in range(1, 8)]
    peers += [dev(vq, lax.rem(z + t // 4, 2) * 4 + y_of[t % 4]) for t in range(1, 8)]
    peers += [
        dev(zh * 8 + lax.rem(e // 2 + t // 2, 4) * 2 + z, lax.rem(z + t, 2) * 4 + y) for t in range(1, 8)
    ]
    peers += [dev(z_ring[t], m) for t in range(1, 4)]
    peers += [dev(vprev, vm), dev(vnext, vm)]
    peers += [place(vnext, x) for x in range(4)] + [place(vprev, 4 + x) for x in range(4)]

    def greet(peer, times):
        pl.semaphore_signal(barrier, inc=times, device_id=peer, device_id_type=MESH)

    for peer in peers:
        greet(peer, 1)

    @pl.when(jnp.logical_not(stays))
    def _():
        greet(dev(vq, m), 2)

    amp_copy = pltpu.make_async_copy(amp_hbm, amp, amp_sem)
    amp_copy.start()

    sub = lax.broadcasted_iota(jnp.int32, (8, 64), 0)
    wanted = jnp.zeros((8, 64), jnp.int32)
    for j in range(8):
        wanted = jnp.where(sub == j, adv_ref[j], wanted)
    owned = (wanted == m * 64 + lax.broadcasted_iota(jnp.int32, (8, 64), 1)).astype(F32).astype(BF16)
    for x in range(4):
        for row in range(2):
            ids = slab_ref[x, row : row + 1, :]
            vol = jnp.zeros((1, 128), F32)
            for level in range(8):
                vol = jnp.where(ids == level, vol_ref[level], vol)
            vol = vol * (0.5 * scale)
            for d in range(3):
                part[row * 4 + x, d] = vol * jnp.dot(owned, u_ref[row, d * 4 + x], preferred_element_type=F32)
    pl.semaphore_wait(barrier, jnp.where(stays, len(peers), len(peers) + 2))

    def piece(ref, p):
        return ref.at[p // 2, pl.ds((p % 2) * 6, 6)]

    def rs_copy(t):
        n = n_ring[t]
        return rcopy(part.at[n], rs_buf.at[m], rs_s.at[t], rs_r.at[m], place(core - z + vq, n))

    for t in range(1, 8):
        rs_copy(t).start()

    @pl.when(stays)
    def _():
        pltpu.make_async_copy(part.at[vm], rs_buf.at[m], rs_r.at[m]).start()
        for p in range(4):
            pltpu.make_async_copy(piece(u_ref, p), piece(ub, p), own_r.at[p]).start()

    def swap(p):
        return rcopy(piece(u_ref, p), piece(ub, p), own_s.at[p], own_r.at[p], dev(vq, vm))

    @pl.when(jnp.logical_not(stays))
    def _():
        rs_copy(0).start()
        for p in range(4):
            swap(p).start()

    up_y = place(vq, core * 4 + ynext)
    down_y = place(vq, core * 4 + yprev)
    to_core = place(vq, (1 - core) * 4 + y)

    def move(src, slot, p, target):
        return rcopy(piece(src, p), piece(blk.at[slot], p), bulk_s.at[slot * 4 + p], bulk_r.at[slot * 4 + p], target)

    started = []

    def go(src, slot, p, target):
        copy = move(src, slot, p, target)
        copy.start()
        started.append(copy)

    def arrived(slot, p):
        move(u_ref, slot, p, here).wait_recv()

    def start_own(p):
        swap(p).wait_recv()
        go(ub, 0, p, up_y)
        go(ub, 1, p, down_y)
        go(ub, 2, p, to_core)

    halo = [
        rcopy(u_ref.at[0], hal.at[1], halo_s.at[0], halo_r.at[0], place(qprev, m)),
        rcopy(u_ref.at[1], hal.at[0], halo_s.at[1], halo_r.at[1], place(qnext, m)),
    ]
    start_own(0)
    start_own(1)
    halo[0].start()
    halo[1].start()

    total = None
    for n in range(8):
        rcopy(part.at[n], rs_buf.at[n], rs_s.at[n], rs_r.at[n], here).wait_recv()
        total = rs_buf[n] if total is None else total + rs_buf[n]
    h_ref[vm] = total

    def ag_copy(t, block):
        return rcopy(h_ref.at[block], h_ref.at[block], ag_s.at[t], ag_r.at[block], place(vq, n_ring[t]))

    vside = jnp.where(core == 0, vprev, vnext)

    def hy_copy(t):
        return rcopy(
            h_ref.at[vm, 1], hyh.at[1 - core, y], hy_s.at[t], hy_r.at[(1 - core) * 4 + y], place(vside, n_ring[t])
        )

    for t in range(8):
        if t > 0:
            ag_copy(t, vm).start()
        hy_copy(t).start()
    start_own(2)
    start_own(3)

    def shift(k, carry):
        for row in range(2):
            tile = ub[row, k].astype(F32)
            up[row, k] = pltpu.roll(tile, 127, 1).astype(BF16)
            um[row, k] = pltpu.roll(tile, 1, 1).astype(BF16)
        return carry

    lax.fori_loop(0, 12, shift, 0)

    def pick_modes(k, carry):
        at = pl.ds(pl.multiple_of(k * 256, 256), 256)
        rows = lax.broadcasted_iota(jnp.int32, (512, 256), 0)
        onehot[:, at] = (rows == pmode_ref[:, at]).astype(F32).astype(BF16)
        return carry

    lax.fori_loop(0, 8, pick_modes, 0)
    mask[...] = (lax.broadcasted_iota(jnp.int32, (8, 2048), 0) == padv_ref[...]).astype(F32)

    for t in range(1, 8):
        ag_copy(t, n_ring[t]).wait_recv()
    for n in range(8):
        hzp[n] = pltpu.roll(h_ref[n, 2], 127, 1)
        hzm[n] = pltpu.roll(h_ref[n, 2], 1, 1)

    for p in (0, 1):
        arrived(0, p)
        go(blk.at[0], 5, p, up_y)
        go(blk.at[0], 3, p, to_core)
        arrived(1, p)
        go(blk.at[1], 4, p, to_core)
    for p in (2, 3):
        arrived(1, p)
        go(blk.at[1], 5, p, down_y)
        go(blk.at[1], 4, p, to_core)
        arrived(0, p)
        go(blk.at[0], 3, p, to_core)

    amp_copy.wait()

    def split_amp(k, carry):
        at = pl.ds(pl.multiple_of(k * 32, 32), 32)
        value = amp[at]
        hi = value.astype(BF16)
        amp_hi[at] = hi
        amp_lo[at] = (value - hi.astype(F32)).astype(BF16)
        return carry

    lax.fori_loop(0, 64, split_amp, 0)

    halo[0].wait_recv()
    halo[1].wait_recv()
    for i in range(2):
        for x in range(4):
            rcopy(hyh.at[i, x], hyh.at[i, x], hy_s.at[x], hy_r.at[i * 4 + x], here).wait_recv()

    first_ok = jnp.where(vq == 0, 0.0, 1.0)
    last_ok = jnp.where(vq == 31, 0.0, 1.0)

    def build(row, c, carry_in):
        def one(x, carry):
            xp = lax.rem(x + 1, 4)
            xm = lax.rem(x + 3, 4)
            at, atp, atm = c * 4 + x, c * 4 + xp, c * 4 + xm
            n = row * 4 + x
            for g in range(2):
                cut = pl.ds(g * 32, 32)
                uxp = ub[row, atp, cut].astype(F32)
                uxm = ub[row, atm, cut].astype(F32)
                uzp = up[row, at, cut].astype(F32)
                uzm = um[row, at, cut].astype(F32)
                if row == 0:
                    uyp = ub[1, at, cut].astype(F32)
                    uym = hal[0, at, cut].astype(F32) * first_ok
                else:
                    uyp = hal[1, at, cut].astype(F32) * last_ok
                    uym = ub[0, at, cut].astype(F32)
                for j in range(8):
                    js = slice(j, j + 1)
                    hyp = h_ref[4 + x, 1, js] if row == 0 else hyh[1, x, js]
                    hym = hyh[0, x, js] if row == 0 else h_ref[x, 1, js]
                    qq = h_ref[row * 4 + xm, 0, js] * uxm - h_ref[row * 4 + xp, 0, js] * uxp
                    qq = qq + (hym * uym - hyp * uyp)
                    qq = qq + (hzm[n, js] * uzm - hzp[n, js] * uzp)
                    lines = pl.ds(j * 64 + g * 32, 32)
                    q_ref[row, at, lines] = qq.astype(BF16)
            return carry

        return lax.fori_loop(0, 4, one, carry_in)

    for row in range(2):
        lax.fori_loop(0, 3, functools.partial(build, row), 0)
        for p in (2 * row, 2 * row + 1):
            arrived(5, p)
            go(blk.at[5], 6, p, to_core)

    def x_copy(n, t):
        return rcopy(
            tb.at[n, :, e_ring[t]], xbuf.at[n, e // 2 * 2 + z], x_s.at[n, t], x_r.at[n, e // 2 * 2 + z],
            dev(zh * 8 + e_ring[t], vm),
        )

    def send_batch(n):
        for k in range(2):
            tb[n, :, :, :, pl.ds(k * 128, 128)] = tf[k].astype(BF16).reshape(4, 8, 16, 128)

        @pl.when(stays)
        def _():
            slot = e // 2 * 2 + z
            pltpu.make_async_copy(tb.at[n, :, e], xbuf.at[n, slot], x_r.at[n, slot]).start()

        @pl.when(jnp.logical_not(stays))
        def _():
            x_copy(n, 0).start()

        for t in range(1, 8):
            x_copy(n, t).start()

    def products(n, parts):
        total = None
        for r in range(2):
            pair = jnp.concatenate(
                [jnp.concatenate([ref[r, k] for k in range(12)], axis=1) for ref in parts], axis=0
            )
            left = jnp.concatenate([q_ref[r, k] for k in range(12)], axis=1)
            value = lax.dot_general(left, pair, NT, preferred_element_type=F32)
            total = value if total is None else total + value
        for j in range(8):
            for k in range(2):
                tf[k, pl.ds(j, 64, stride=8), :] = total[j * 64 : (j + 1) * 64, k * 128 : (k + 1) * 128]
        send_batch(n)

    def z_copy(n, t):
        return rcopy(zsrc.at[n, lax.rem(zh + t, 4)], zbuf.at[n, t], z_s.at[n, t], z_r.at[n, t], dev(z_ring[t], m))

    def gather_batch(n):
        total = None
        for t in range(8):
            rcopy(xbuf.at[n, t], xbuf.at[n, t], x_s.at[n, t], x_r.at[n, t], here).wait_recv()
            value = xbuf[n, t].astype(F32)
            total = value if total is None else total + value
        zsrc[n] = total
        for t in range(1, 4):
            z_copy(n, t).start()

    for p in range(4):
        arrived(2, p)
    products(0, (ub, blk.at[2], blk.at[0], blk.at[1]))
    for p in range(4):
        arrived(3, p)
        arrived(4, p)
        arrived(6, p)
    products(1, (blk.at[3], blk.at[4], blk.at[5], blk.at[6]))
    gather_batch(0)
    gather_batch(1)

    blocks = [
        (m, (1 - z) * 4 + y, z * 4 + yprev, z * 4 + ynext),
        ((1 - z) * 4 + yprev, (1 - z) * 4 + ynext, z * 4 + yfar, (1 - z) * 4 + yfar),
    ]
    for n in range(2):
        value = zsrc[n, zh]
        for t in range(1, 4):
            z_copy(n, t).wait_recv()
            value = value + zbuf[n, t]
        for k in range(2):
            pair = value[:, k * 128 : (k + 1) * 128]
            fin[blocks[n][2 * k]] = pair
            fin[blocks[n][2 * k + 1]] = pltpu.roll(pair, 64, 1)

    low = lax.broadcasted_iota(jnp.int32, (16, 128), 1) < 64
    columns = []
    for t in range(4):
        columns.append(jnp.where(low, fin[2 * t], pltpu.roll(fin[2 * t + 1], 64, 1)))
    tensor = jnp.concatenate(columns, axis=1)
    out_ref[...] = tensor
    top = tensor.astype(BF16)
    rest = (tensor - top.astype(F32)).astype(BF16)
    chosen = jnp.dot(jnp.concatenate([top, rest], axis=0), onehot[...], preferred_element_type=F32)
    chosen = chosen[:16] + chosen[16:]
    first = jnp.sum(chosen[:8] * mask[...], axis=0, keepdims=True)
    second = jnp.sum(chosen[8:] * mask[...], axis=0, keepdims=True)
    rows = lax.broadcasted_iota(jnp.int32, (16, 2048), 0)
    both = jnp.where(lax.rem(rows, 2) == 0, first, second)
    both_hi = both.astype(BF16).astype(F32)
    stacked = jnp.where(rows < 2, both_hi, jnp.where(rows < 4, both - both_hi, 0.0)).astype(BF16)
    answer = jnp.dot(stacked, amp_hi[...], preferred_element_type=F32)
    answer = answer + jnp.dot(stacked, amp_lo[...], preferred_element_type=F32)
    resp_ref[...] = answer[0:2] + answer[2:4]

    for t in range(1, 8):
        rs_copy(t).wait_send()
        ag_copy(t, vm).wait_send()
    for t in range(8):
        hy_copy(t).wait_send()
    for copy in started + halo:
        copy.wait_send()
    for n in range(2):
        for t in range(1, 8):
            x_copy(n, t).wait_send()
        for t in range(1, 4):
            z_copy(n, t).wait_send()

    @pl.when(jnp.logical_not(stays))
    def _():
        rs_copy(0).wait_send()
        for p in range(4):
            swap(p).wait_send()
        for n in range(2):
            x_copy(n, 0).wait_send()


def finish(tensor_ref, response_ref, out_ref, resp_ref):
    out_ref[...] = tensor_ref[...]
    resp_ref[...] = response_ref[...]


def shards(pod_modes, slab_map, slab_volume, advect_index, pair_adv, pair_mode, pair_amp):
    cells = pod_modes.shape[2] * pod_modes.shape[3] * lax.axis_size("cell") * pod_modes.shape[4]
    u = jnp.transpose(pod_modes, (3, 0, 2, 1, 4)).reshape(2, 12, 64, 128)
    vmem = pl.BlockSpec(memory_space=pltpu.VMEM)
    smem = pl.BlockSpec(memory_space=pltpu.SMEM)
    dma = pltpu.SemaphoreType.DMA
    shapes = (jax.ShapeDtypeStruct((16, 512), F32), jax.ShapeDtypeStruct((2, 1024), F32))
    results = pl.pallas_call(
        functools.partial(kernel, float(cells) ** -0.5),
        out_shape=shapes,
        in_specs=[vmem, vmem, smem, smem, vmem, vmem, pl.BlockSpec(memory_space=pl.ANY)],
        out_specs=(vmem, vmem),
        scratch_shapes=[
            pltpu.VMEM((2, 12, 64, 128), BF16),
            pltpu.VMEM((7, 2, 12, 64, 128), BF16),
            pltpu.VMEM((2, 12, 64, 128), BF16),
            pltpu.VMEM((2, 12, 64, 128), BF16),
            pltpu.VMEM((2, 12, 64, 128), BF16),
            pltpu.VMEM((2, 12, 512, 128), BF16),
            pltpu.VMEM((8, 3, 8, 128), F32),
            pltpu.VMEM((8, 3, 8, 128), F32),
            pltpu.VMEM((8, 3, 8, 128), F32),
            pltpu.VMEM((2, 4, 8, 128), F32),
            pltpu.VMEM((8, 8, 128), F32),
            pltpu.VMEM((8, 8, 128), F32),
            pltpu.VMEM((2, 512, 128), F32),
            pltpu.VMEM((2, 4, 8, 16, 256), BF16),
            pltpu.VMEM((2, 8, 4, 16, 256), BF16),
            pltpu.VMEM((2, 4, 16, 256), F32),
            pltpu.VMEM((2, 4, 16, 256), F32),
            pltpu.VMEM((8, 16, 128), F32),
            pltpu.VMEM((2048, 1024), F32),
            pltpu.VMEM((2048, 1024), BF16),
            pltpu.VMEM((2048, 1024), BF16),
            pltpu.VMEM((512, 2048), BF16),
            pltpu.VMEM((8, 2048), F32),
            dma((8,)), dma((8,)), dma((8,)), dma((8,)),
            dma((4,)), dma((4,)), dma((28,)), dma((28,)), dma((2,)), dma((2,)), dma((8,)), dma((8,)),
            dma((2, 8)), dma((2, 8)), dma((2, 4)), dma((2, 4)), dma,
        ],
        compiler_params=pltpu.CompilerParams(
            collective_id=0, has_side_effects=True, vmem_limit_bytes=60 * 2**20
        ),
        name="pod_tensor",
    )(
        u, slab_map, slab_volume, advect_index,
        pair_adv.reshape(1, -1), pair_mode.reshape(1, -1), pair_amp,
    )
    tensor, response = pl.pallas_call(
        finish, out_shape=shapes, in_specs=[vmem, vmem], out_specs=(vmem, vmem), name="finish"
    )(*results)
    return tensor.reshape(2, 8, 512), response


def solution(mesh):
    in_specs = (P(None, "mode", None, "cell", None), P(None, "cell", None), P(), P(), P(), P(), P())
    out_specs = (P(("mode", "cell"), None, None), P(("mode", "cell"), None))
    return jax.shard_map(shards, mesh=mesh, in_specs=in_specs, out_specs=out_specs, check_vma=False)
```

```python
import functools
import jax
import jax.numpy as jnp
from jax import lax
from jax.experimental import pallas as pl
from jax.experimental.pallas import tpu as pltpu
from jax.sharding import PartitionSpec as P

MESH = pl.DeviceIdType.MESH
F32 = jnp.float32
BF16 = jnp.bfloat16
NT = (((1,), (1,)), ((), ()))


def kernel(
    scale,
    u_ref, slab_ref, vol_ref, adv_ref, padv_ref, pmode_ref, amp_hbm,
    out_ref, resp_ref,
    ub, blk, hal, up, um, q_ref,
    part, rs_buf, h_ref, hyh, hzp, hzm,
    tf, tb, xbuf, zsrc, zbuf, fin,
    amp, amp_hi, amp_lo, onehot, mask,
    rs_s, rs_r, ag_s, ag_r, own_s, own_r, bulk_s, bulk_r, halo_s, halo_r, hy_s, hy_r, x_s, x_r, z_s, z_r, amp_sem, token,
):
    q = lax.axis_index("cell")
    m = lax.axis_index("mode")
    core = lax.rem(q, 2)
    e = lax.rem(q, 8)
    zh = q // 8
    z = m // 4
    y = lax.rem(m, 4)
    zb = 1 - z
    stays = core == z
    vq = q - core + z
    vm = core * 4 + y
    ynext = lax.rem(y + 1, 4)
    yprev = lax.rem(y + 3, 4)
    yfar = lax.rem(y + 2, 4)

    def place(cell, block):
        return dev(cell - lax.rem(cell, 2) + block // 4, lax.rem(cell, 2) * 4 + lax.rem(block, 4))

    def dev(cell, mode):
        return {"cell": cell, "mode": mode}

    def rcopy(src, dst, send, recv, target):
        return pltpu.make_async_remote_copy(
            src_ref=src, dst_ref=dst, send_sem=send, recv_sem=recv,
            device_id=target, device_id_type=MESH,
        )

    here = dev(q, m)
    n_ring = [lax.rem(vm + t, 8) for t in range(8)]
    e_ring = [lax.rem(e + t, 8) for t in range(8)]
    z_ring = [lax.rem(zh + t, 4) * 8 + e for t in range(4)]
    vprev = lax.rem(vq + 31, 32)
    vnext = lax.rem(vq + 1, 32)
    qprev = lax.rem(q + 31, 32)
    qnext = lax.rem(q + 1, 32)

    barrier = pltpu.get_barrier_semaphore()
    z_up = dev(lax.rem(zh + z, 4) * 8 + e, zb * 4 + y)
    z_down = dev(lax.rem(zh + 3 + z, 4) * 8 + e, zb * 4 + y)
    y_of = [lax.rem(y + t, 4) for t in range(4)]
    peers = [place(vq, n_ring[t]) for t in range(1, 8)]
    peers += [dev(vq, lax.rem(z + t // 4, 2) * 4 + y_of[t % 4]) for t in range(1, 8)]
    peers += [
        dev(zh * 8 + lax.rem(e // 2 + t // 2, 4) * 2 + z, lax.rem(z + t, 2) * 4 + y) for t in range(1, 8)
    ]
    peers += [z_up, z_down]
    peers += [dev(vprev, vm), dev(vnext, vm)]
    peers += [place(vnext, x) for x in range(4)] + [place(vprev, 4 + x) for x in range(4)]

    def greet(peer, times):
        pl.semaphore_signal(barrier, inc=times, device_id=peer, device_id_type=MESH)

    for peer in peers:
        greet(peer, 1)

    @pl.when(jnp.logical_not(stays))
    def _():
        greet(dev(vq, m), 2)

    amp_copy = pltpu.make_async_copy(amp_hbm, amp, amp_sem)
    amp_copy.start()

    sub = lax.broadcasted_iota(jnp.int32, (8, 64), 0)
    wanted = jnp.zeros((8, 64), jnp.int32)
    for j in range(8):
        wanted = jnp.where(sub == j, adv_ref[j], wanted)
    owned = (wanted == m * 64 + lax.broadcasted_iota(jnp.int32, (8, 64), 1)).astype(F32).astype(BF16)
    for x in range(4):
        for row in range(2):
            ids = slab_ref[x, row : row + 1, :]
            vol = jnp.zeros((1, 128), F32)
            for level in range(8):
                vol = jnp.where(ids == level, vol_ref[level], vol)
            vol = vol * (0.5 * scale)
            for d in range(3):
                part[row * 4 + x, d] = vol * jnp.dot(owned, u_ref[row, d * 4 + x], preferred_element_type=F32)
    pl.semaphore_wait(barrier, jnp.where(stays, len(peers), len(peers) + 2))

    def piece(ref, p):
        return ref.at[p // 2, pl.ds((p % 2) * 6, 6)]

    def pass_token(k):
        pl.semaphore_signal(token.at[k, 0], inc=1, device_id=z_up, device_id_type=MESH)
        pl.semaphore_signal(token.at[k, 1], inc=1, device_id=z_down, device_id_type=MESH)

    def take_token(k):
        pl.semaphore_wait(token.at[k, 0], 1)
        pl.semaphore_wait(token.at[k, 1], 1)

    pass_token(0)

    def rs_copy(t):
        n = n_ring[t]
        return rcopy(part.at[n], rs_buf.at[m], rs_s.at[t], rs_r.at[m], place(core - z + vq, n))

    for t in range(1, 8):
        rs_copy(t).start()

    @pl.when(stays)
    def _():
        pltpu.make_async_copy(part.at[vm], rs_buf.at[m], rs_r.at[m]).start()
        for p in range(4):
            pltpu.make_async_copy(piece(u_ref, p), piece(ub, p), own_r.at[p]).start()

    def swap(p):
        return rcopy(piece(u_ref, p), piece(ub, p), own_s.at[p], own_r.at[p], dev(vq, vm))

    @pl.when(jnp.logical_not(stays))
    def _():
        rs_copy(0).start()
        for p in (0, 2, 1, 3):
            swap(p).start()

    up_y = place(vq, core * 4 + ynext)
    down_y = place(vq, core * 4 + yprev)
    to_core = place(vq, (1 - core) * 4 + y)

    def move(src, slot, p, target):
        return rcopy(piece(src, p), piece(blk.at[slot], p), bulk_s.at[slot * 4 + p], bulk_r.at[slot * 4 + p], target)

    started = []

    def go(src, slot, p, target):
        copy = move(src, slot, p, target)
        copy.start()
        started.append(copy)

    def arrived(slot, p):
        move(u_ref, slot, p, here).wait_recv()

    def start_first(p):
        swap(p).wait_recv()
        go(ub, 0, p, up_y)
        swap(p + 2).wait_recv()
        go(ub, 1, p + 2, down_y)

    def start_rest(p):
        go(ub, 0, p + 2, up_y)
        go(ub, 1, p, down_y)
        go(ub, 2, p, to_core)
        go(ub, 2, p + 2, to_core)

    halo = [
        rcopy(u_ref.at[0], hal.at[1], halo_s.at[0], halo_r.at[0], place(qprev, m)),
        rcopy(u_ref.at[1], hal.at[0], halo_s.at[1], halo_r.at[1], place(qnext, m)),
    ]
    for p in range(2):
        start_first(p)
    for p in range(2):
        start_rest(p)

    total = None
    for n in range(8):
        rcopy(part.at[n], rs_buf.at[n], rs_s.at[n], rs_r.at[n], here).wait_recv()
        total = rs_buf[n] if total is None else total + rs_buf[n]
    h_ref[vm] = total
    take_token(0)
    pass_token(1)

    def ag_copy(t, block):
        return rcopy(h_ref.at[block], h_ref.at[block], ag_s.at[t], ag_r.at[block], place(vq, n_ring[t]))

    vside = jnp.where(core == 0, vprev, vnext)

    def hy_copy(t):
        return rcopy(
            h_ref.at[vm, 1], hyh.at[1 - core, y], hy_s.at[t], hy_r.at[(1 - core) * 4 + y], place(vside, n_ring[t])
        )

    for t in range(8):
        if t > 0:
            ag_copy(t, vm).start()
        hy_copy(t).start()
    halo[0].start()
    halo[1].start()

    for p in range(2):
        arrived(0, p)
        go(blk.at[0], 5, p, up_y)
        go(blk.at[0], 3, p, to_core)
        arrived(1, p + 2)
        go(blk.at[1], 5, p + 2, down_y)
        go(blk.at[1], 4, p + 2, to_core)

    def shift(k, carry):
        for row in range(2):
            tile = ub[row, k].astype(F32)
            up[row, k] = pltpu.roll(tile, 127, 1).astype(BF16)
            um[row, k] = pltpu.roll(tile, 1, 1).astype(BF16)
        return carry

    lax.fori_loop(0, 12, shift, 0)

    for t in range(1, 8):
        ag_copy(t, n_ring[t]).wait_recv()
    take_token(1)
    pass_token(2)
    for n in range(8):
        hzp[n] = pltpu.roll(h_ref[n, 2], 127, 1)
        hzm[n] = pltpu.roll(h_ref[n, 2], 1, 1)

    for p in range(2):
        arrived(0, p + 2)
        go(blk.at[0], 3, p + 2, to_core)
        arrived(1, p)
        go(blk.at[1], 4, p, to_core)

    halo[0].wait_recv()
    halo[1].wait_recv()
    for i in range(2):
        for x in range(4):
            rcopy(hyh.at[i, x], hyh.at[i, x], hy_s.at[x], hy_r.at[i * 4 + x], here).wait_recv()

    first_ok = jnp.where(vq == 0, 0.0, 1.0)
    last_ok = jnp.where(vq == 31, 0.0, 1.0)

    def build(row, c, carry_in):
        def one(x, carry):
            xp = lax.rem(x + 1, 4)
            xm = lax.rem(x + 3, 4)
            at, atp, atm = c * 4 + x, c * 4 + xp, c * 4 + xm
            n = row * 4 + x
            for g in range(2):
                cut = pl.ds(g * 32, 32)
                uxp = ub[row, atp, cut].astype(F32)
                uxm = ub[row, atm, cut].astype(F32)
                uzp = up[row, at, cut].astype(F32)
                uzm = um[row, at, cut].astype(F32)
                if row == 0:
                    uyp = ub[1, at, cut].astype(F32)
                    uym = hal[0, at, cut].astype(F32) * first_ok
                else:
                    uyp = hal[1, at, cut].astype(F32) * last_ok
                    uym = ub[0, at, cut].astype(F32)
                for j in range(8):
                    js = slice(j, j + 1)
                    hyp = h_ref[4 + x, 1, js] if row == 0 else hyh[1, x, js]
                    hym = hyh[0, x, js] if row == 0 else h_ref[x, 1, js]
                    qq = h_ref[row * 4 + xm, 0, js] * uxm - h_ref[row * 4 + xp, 0, js] * uxp
                    qq = qq + (hym * uym - hyp * uyp)
                    qq = qq + (hzm[n, js] * uzm - hzp[n, js] * uzp)
                    lines = pl.ds(j * 64 + g * 32, 32)
                    q_ref[row, at, lines] = qq.astype(BF16)
            return carry

        return lax.fori_loop(0, 4, one, carry_in)

    for row in range(2):
        lax.fori_loop(0, 3, functools.partial(build, row), 0)

    def x_copy(n, t):
        return rcopy(
            tb.at[n, :, e_ring[t]], xbuf.at[n, e // 2 * 2 + z], x_s.at[n, t], x_r.at[n, e // 2 * 2 + z],
            dev(zh * 8 + e_ring[t], vm),
        )

    def send_batch(n):
        tb[n] = tf[n].astype(BF16).reshape(4, 8, 16, 128)

        @pl.when(stays)
        def _():
            slot = e // 2 * 2 + z
            pltpu.make_async_copy(tb.at[n, :, e], xbuf.at[n, slot], x_r.at[n, slot]).start()

        @pl.when(jnp.logical_not(stays))
        def _():
            x_copy(n, 0).start()

        for t in range(1, 8):
            x_copy(n, t).start()

    def products(first, parts):
        total = None
        for r in range(2):
            pair = jnp.concatenate(
                [jnp.concatenate([ref[r, k] for k in range(12)], axis=1) for ref in parts], axis=0
            )
            left = jnp.concatenate([q_ref[r, k] for k in range(12)], axis=1)
            value = lax.dot_general(left, pair, NT, preferred_element_type=F32)
            total = value if total is None else total + value
        for k in range(len(parts) // 2):
            for j in range(8):
                tf[first + k, pl.ds(j, 64, stride=8), :] = total[j * 64 : (j + 1) * 64, k * 128 : (k + 1) * 128]
            send_batch(first + k)

    def z_copy(n, t):
        return rcopy(zsrc.at[n, lax.rem(zh + t, 4)], zbuf.at[n, t], z_s.at[n, t], z_r.at[n, t], dev(z_ring[t], m))

    def gather_batch(n):
        total = None
        for t in range(8):
            rcopy(xbuf.at[n, t], xbuf.at[n, t], x_s.at[n, t], x_r.at[n, t], here).wait_recv()
            value = xbuf[n, t].astype(F32)
            total = value if total is None else total + value
        zsrc[n] = total
        for t in range(1, 4):
            z_copy(n, t).start()

    for p in range(4):
        arrived(2, p)
    for p in (0, 2, 1, 3):
        arrived(5, p)
        go(blk.at[5], 6, p, to_core)
    products(0, (ub, blk.at[2], blk.at[0], blk.at[1]))
    for p in range(4):
        arrived(3, p)
        arrived(4, p)
    products(2, (blk.at[3], blk.at[4]))
    for p in range(4):
        arrived(6, p)
    products(3, (blk.at[5], blk.at[6]))
    def pick_modes(k, carry):
        at = pl.ds(pl.multiple_of(k * 256, 256), 256)
        rows = lax.broadcasted_iota(jnp.int32, (512, 256), 0)
        onehot[:, at] = (rows == pmode_ref[:, at]).astype(F32).astype(BF16)
        return carry

    lax.fori_loop(0, 8, pick_modes, 0)
    mask[...] = (lax.broadcasted_iota(jnp.int32, (8, 2048), 0) == padv_ref[...]).astype(F32)

    amp_copy.wait()

    def split_amp(k, carry):
        at = pl.ds(pl.multiple_of(k * 32, 32), 32)
        value = amp[at]
        hi = value.astype(BF16)
        amp_hi[at] = hi
        amp_lo[at] = (value - hi.astype(F32)).astype(BF16)
        return carry

    lax.fori_loop(0, 64, split_amp, 0)

    for t in range(1, 8):
        rs_copy(t).wait_send()
        ag_copy(t, vm).wait_send()
    for t in range(8):
        hy_copy(t).wait_send()
    for copy in started + halo:
        copy.wait_send()
    take_token(2)
    for n in range(4):
        gather_batch(n)
    for n in range(4):
        for t in range(1, 8):
            x_copy(n, t).wait_send()

    blocks = [
        (m, zb * 4 + y),
        (z * 4 + yprev, z * 4 + ynext),
        (zb * 4 + yprev, zb * 4 + ynext),
        (z * 4 + yfar, zb * 4 + yfar),
    ]
    for n in range(4):
        value = zsrc[n, zh]
        for t in range(1, 4):
            z_copy(n, t).wait_recv()
            value = value + zbuf[n, t]
        fin[blocks[n][0]] = value
        fin[blocks[n][1]] = pltpu.roll(value, 64, 1)

    low = lax.broadcasted_iota(jnp.int32, (16, 128), 1) < 64
    columns = []
    for t in range(4):
        columns.append(jnp.where(low, fin[2 * t], pltpu.roll(fin[2 * t + 1], 64, 1)))
    tensor = jnp.concatenate(columns, axis=1)
    out_ref[...] = tensor
    top = tensor.astype(BF16)
    rest = (tensor - top.astype(F32)).astype(BF16)
    chosen = jnp.dot(jnp.concatenate([top, rest], axis=0), onehot[...], preferred_element_type=F32)
    chosen = chosen[:16] + chosen[16:]
    first = jnp.sum(chosen[:8] * mask[...], axis=0, keepdims=True)
    second = jnp.sum(chosen[8:] * mask[...], axis=0, keepdims=True)
    rows = lax.broadcasted_iota(jnp.int32, (16, 2048), 0)
    both = jnp.where(lax.rem(rows, 2) == 0, first, second)
    both_hi = both.astype(BF16).astype(F32)
    stacked = jnp.where(rows < 2, both_hi, jnp.where(rows < 4, both - both_hi, 0.0)).astype(BF16)
    answer = jnp.dot(stacked, amp_hi[...], preferred_element_type=F32)
    answer = answer + jnp.dot(stacked, amp_lo[...], preferred_element_type=F32)
    resp_ref[...] = answer[0:2] + answer[2:4]

    for n in range(4):
        for t in range(1, 4):
            z_copy(n, t).wait_send()

    @pl.when(jnp.logical_not(stays))
    def _():
        rs_copy(0).wait_send()
        for p in range(4):
            swap(p).wait_send()
        for n in range(4):
            x_copy(n, 0).wait_send()


def finish(tensor_ref, response_ref, out_ref, resp_ref):
    out_ref[...] = tensor_ref[...]
    resp_ref[...] = response_ref[...]


def shards(pod_modes, slab_map, slab_volume, advect_index, pair_adv, pair_mode, pair_amp):
    cells = pod_modes.shape[2] * pod_modes.shape[3] * lax.axis_size("cell") * pod_modes.shape[4]
    u = jnp.transpose(pod_modes, (3, 0, 2, 1, 4)).reshape(2, 12, 64, 128)
    vmem = pl.BlockSpec(memory_space=pltpu.VMEM)
    smem = pl.BlockSpec(memory_space=pltpu.SMEM)
    dma = pltpu.SemaphoreType.DMA
    shapes = (jax.ShapeDtypeStruct((16, 512), F32), jax.ShapeDtypeStruct((2, 1024), F32))
    results = pl.pallas_call(
        functools.partial(kernel, float(cells) ** -0.5),
        out_shape=shapes,
        in_specs=[vmem, vmem, smem, smem, vmem, vmem, pl.BlockSpec(memory_space=pl.ANY)],
        out_specs=(vmem, vmem),
        scratch_shapes=[
            pltpu.VMEM((2, 12, 64, 128), BF16),
            pltpu.VMEM((7, 2, 12, 64, 128), BF16),
            pltpu.VMEM((2, 12, 64, 128), BF16),
            pltpu.VMEM((2, 12, 64, 128), BF16),
            pltpu.VMEM((2, 12, 64, 128), BF16),
            pltpu.VMEM((2, 12, 512, 128), BF16),
            pltpu.VMEM((8, 3, 8, 128), F32),
            pltpu.VMEM((8, 3, 8, 128), F32),
            pltpu.VMEM((8, 3, 8, 128), F32),
            pltpu.VMEM((2, 4, 8, 128), F32),
            pltpu.VMEM((8, 8, 128), F32),
            pltpu.VMEM((8, 8, 128), F32),
            pltpu.VMEM((4, 512, 128), F32),
            pltpu.VMEM((4, 4, 8, 16, 128), BF16),
            pltpu.VMEM((4, 8, 4, 16, 128), BF16),
            pltpu.VMEM((4, 4, 16, 128), F32),
            pltpu.VMEM((4, 4, 16, 128), F32),
            pltpu.VMEM((8, 16, 128), F32),
            pltpu.VMEM((2048, 1024), F32),
            pltpu.VMEM((2048, 1024), BF16),
            pltpu.VMEM((2048, 1024), BF16),
            pltpu.VMEM((512, 2048), BF16),
            pltpu.VMEM((8, 2048), F32),
            dma((8,)), dma((8,)), dma((8,)), dma((8,)),
            dma((4,)), dma((4,)), dma((28,)), dma((28,)), dma((2,)), dma((2,)), dma((8,)), dma((8,)),
            dma((4, 8)), dma((4, 8)), dma((4, 4)), dma((4, 4)), dma,
            pltpu.SemaphoreType.REGULAR((3, 2)),
        ],
        compiler_params=pltpu.CompilerParams(
            collective_id=0, has_side_effects=True, vmem_limit_bytes=60 * 2**20
        ),
        name="pod_tensor",
    )(
        u, slab_map, slab_volume, advect_index,
        pair_adv.reshape(1, -1), pair_mode.reshape(1, -1), pair_amp,
    )
    tensor, response = pl.pallas_call(
        finish, out_shape=shapes, in_specs=[vmem, vmem], out_specs=(vmem, vmem), name="finish"
    )(*results)
    return tensor.reshape(2, 8, 512), response


def solution(mesh):
    in_specs = (P(None, "mode", None, "cell", None), P(None, "cell", None), P(), P(), P(), P(), P())
    out_specs = (P(("mode", "cell"), None, None), P(("mode", "cell"), None))
    return jax.shard_map(shards, mesh=mesh, in_specs=in_specs, out_specs=out_specs, check_vma=False)
```

```python
import functools
import jax
import jax.numpy as jnp
from jax import lax
from jax.experimental import pallas as pl
from jax.experimental.pallas import tpu as pltpu
from jax.sharding import PartitionSpec as P

MESH = pl.DeviceIdType.MESH
F32 = jnp.float32
BF16 = jnp.bfloat16
NT = (((1,), (1,)), ((), ()))


def kernel(
    scale,
    u_ref, slab_ref, vol_ref, adv_ref, padv_ref, pmode_ref, amp_hbm,
    out_ref, resp_ref,
    ub, blk, hal, up, um, q_ref,
    part, rs_buf, h_ref, hyh, hzp, hzm,
    tf, tb, xbuf, zsrc, zbuf, fin,
    amp, amp_hi, amp_lo, onehot, mask,
    rs_s, rs_r, ag_s, ag_r, own_s, own_r, bulk_s, bulk_r, halo_s, halo_r, hy_s, hy_r, x_s, x_r, z_s, z_r, amp_sem, token,
):
    q = lax.axis_index("cell")
    m = lax.axis_index("mode")
    core = lax.rem(q, 2)
    e = lax.rem(q, 8)
    zh = q // 8
    z = m // 4
    y = lax.rem(m, 4)
    zb = 1 - z
    stays = core == z
    vq = q - core + z
    vm = core * 4 + y
    ynext = lax.rem(y + 1, 4)
    yprev = lax.rem(y + 3, 4)
    yfar = lax.rem(y + 2, 4)

    def place(cell, block):
        return dev(cell - lax.rem(cell, 2) + block // 4, lax.rem(cell, 2) * 4 + lax.rem(block, 4))

    def dev(cell, mode):
        return {"cell": cell, "mode": mode}

    def rcopy(src, dst, send, recv, target):
        return pltpu.make_async_remote_copy(
            src_ref=src, dst_ref=dst, send_sem=send, recv_sem=recv,
            device_id=target, device_id_type=MESH,
        )

    here = dev(q, m)
    n_ring = [lax.rem(vm + t, 8) for t in range(8)]
    e_ring = [lax.rem(e + t, 8) for t in range(8)]
    z_ring = [lax.rem(zh + t, 4) * 8 + e for t in range(4)]
    vprev = lax.rem(vq + 31, 32)
    vnext = lax.rem(vq + 1, 32)
    qprev = lax.rem(q + 31, 32)
    qnext = lax.rem(q + 1, 32)

    barrier = pltpu.get_barrier_semaphore()
    z_up = dev(lax.rem(zh + z, 4) * 8 + e, zb * 4 + y)
    z_down = dev(lax.rem(zh + 3 + z, 4) * 8 + e, zb * 4 + y)
    y_of = [lax.rem(y + t, 4) for t in range(4)]
    peers = [place(vq, n_ring[t]) for t in range(1, 8)]
    peers += [dev(vq, lax.rem(z + t // 4, 2) * 4 + y_of[t % 4]) for t in range(1, 8)]
    peers += [
        dev(zh * 8 + lax.rem(e // 2 + t // 2, 4) * 2 + z, lax.rem(z + t, 2) * 4 + y) for t in range(1, 8)
    ]
    peers += [z_up, z_down]
    peers += [dev(vprev, vm), dev(vnext, vm)]
    peers += [place(vnext, x) for x in range(4)] + [place(vprev, 4 + x) for x in range(4)]

    def greet(peer, times):
        pl.semaphore_signal(barrier, inc=times, device_id=peer, device_id_type=MESH)

    for peer in peers:
        greet(peer, 1)

    @pl.when(jnp.logical_not(stays))
    def _():
        greet(dev(vq, m), 2)

    amp_copy = pltpu.make_async_copy(amp_hbm, amp, amp_sem)
    amp_copy.start()

    sub = lax.broadcasted_iota(jnp.int32, (8, 64), 0)
    wanted = jnp.zeros((8, 64), jnp.int32)
    for j in range(8):
        wanted = jnp.where(sub == j, adv_ref[j], wanted)
    owned = (wanted == m * 64 + lax.broadcasted_iota(jnp.int32, (8, 64), 1)).astype(F32).astype(BF16)
    for x in range(4):
        for row in range(2):
            ids = slab_ref[x, row : row + 1, :]
            vol = jnp.zeros((1, 128), F32)
            for level in range(8):
                vol = jnp.where(ids == level, vol_ref[level], vol)
            vol = vol * (0.5 * scale)
            for d in range(3):
                part[row * 4 + x, d] = vol * jnp.dot(owned, u_ref[row, d * 4 + x], preferred_element_type=F32)
    pl.semaphore_wait(barrier, jnp.where(stays, len(peers), len(peers) + 2))

    def piece(ref, p):
        return ref.at[p // 2, pl.ds((p % 2) * 6, 6)]

    def pass_token(k):
        pl.semaphore_signal(token.at[k, 0], inc=1, device_id=z_up, device_id_type=MESH)
        pl.semaphore_signal(token.at[k, 1], inc=1, device_id=z_down, device_id_type=MESH)

    def take_token(k):
        pl.semaphore_wait(token.at[k, 0], 1)
        pl.semaphore_wait(token.at[k, 1], 1)

    pass_token(0)

    def rs_copy(t):
        n = n_ring[t]
        return rcopy(part.at[n], rs_buf.at[m], rs_s.at[t], rs_r.at[m], place(core - z + vq, n))

    for t in range(1, 8):
        rs_copy(t).start()

    @pl.when(stays)
    def _():
        pltpu.make_async_copy(part.at[vm], rs_buf.at[m], rs_r.at[m]).start()
        for p in range(4):
            pltpu.make_async_copy(piece(u_ref, p), piece(ub, p), own_r.at[p]).start()

    def swap(p):
        return rcopy(piece(u_ref, p), piece(ub, p), own_s.at[p], own_r.at[p], dev(vq, vm))

    @pl.when(jnp.logical_not(stays))
    def _():
        rs_copy(0).start()
        for p in (0, 2, 1, 3):
            swap(p).start()

    up_y = place(vq, core * 4 + ynext)
    down_y = place(vq, core * 4 + yprev)
    to_core = place(vq, (1 - core) * 4 + y)

    def move(src, slot, p, target):
        return rcopy(piece(src, p), piece(blk.at[slot], p), bulk_s.at[slot * 4 + p], bulk_r.at[slot * 4 + p], target)

    started = []

    def go(src, slot, p, target):
        copy = move(src, slot, p, target)
        copy.start()
        started.append(copy)

    def arrived(slot, p):
        move(u_ref, slot, p, here).wait_recv()

    def start_first(p):
        swap(p).wait_recv()
        go(ub, 0, p, up_y)
        swap(p + 2).wait_recv()
        go(ub, 1, p + 2, down_y)

    def start_rest(p):
        go(ub, 0, p + 2, up_y)
        go(ub, 1, p, down_y)
        go(ub, 2, p, to_core)
        go(ub, 2, p + 2, to_core)

    halo = [
        rcopy(u_ref.at[0], hal.at[1], halo_s.at[0], halo_r.at[0], place(qprev, m)),
        rcopy(u_ref.at[1], hal.at[0], halo_s.at[1], halo_r.at[1], place(qnext, m)),
    ]
    for p in range(2):
        start_first(p)
    for p in range(2):
        start_rest(p)

    total = None
    for n in range(8):
        rcopy(part.at[n], rs_buf.at[n], rs_s.at[n], rs_r.at[n], here).wait_recv()
        total = rs_buf[n] if total is None else total + rs_buf[n]
    h_ref[vm] = total
    take_token(0)
    pass_token(1)

    def ag_copy(t, block):
        return rcopy(h_ref.at[block], h_ref.at[block], ag_s.at[t], ag_r.at[block], place(vq, n_ring[t]))

    vside = jnp.where(core == 0, vprev, vnext)

    def hy_copy(t):
        return rcopy(
            h_ref.at[vm, 1], hyh.at[1 - core, y], hy_s.at[t], hy_r.at[(1 - core) * 4 + y], place(vside, n_ring[t])
        )

    for t in range(8):
        if t > 0:
            ag_copy(t, vm).start()
        hy_copy(t).start()
    halo[0].start()
    halo[1].start()

    for p in range(2):
        arrived(0, p)
        go(blk.at[0], 5, p, up_y)
        go(blk.at[0], 3, p, to_core)
        arrived(1, p + 2)
        go(blk.at[1], 5, p + 2, down_y)
        go(blk.at[1], 4, p + 2, to_core)

    def shift(k, carry):
        for row in range(2):
            tile = ub[row, k].astype(F32)
            up[row, k] = pltpu.roll(tile, 127, 1).astype(BF16)
            um[row, k] = pltpu.roll(tile, 1, 1).astype(BF16)
        return carry

    lax.fori_loop(0, 12, shift, 0)

    for t in range(1, 8):
        ag_copy(t, n_ring[t]).wait_recv()
    take_token(1)
    pass_token(2)
    for n in range(8):
        hzp[n] = pltpu.roll(h_ref[n, 2], 127, 1)
        hzm[n] = pltpu.roll(h_ref[n, 2], 1, 1)

    for p in range(2):
        arrived(0, p + 2)
        go(blk.at[0], 3, p + 2, to_core)
        arrived(1, p)
        go(blk.at[1], 4, p, to_core)

    halo[0].wait_recv()
    halo[1].wait_recv()
    for i in range(2):
        for x in range(4):
            rcopy(hyh.at[i, x], hyh.at[i, x], hy_s.at[x], hy_r.at[i * 4 + x], here).wait_recv()

    first_ok = jnp.where(vq == 0, 0.0, 1.0)
    last_ok = jnp.where(vq == 31, 0.0, 1.0)

    def build(g, row, c, carry_in):
        def one(x, carry):
            xp = lax.rem(x + 1, 4)
            xm = lax.rem(x + 3, 4)
            at, atp, atm = c * 4 + x, c * 4 + xp, c * 4 + xm
            n = row * 4 + x
            cut = pl.ds(g * 32, 32)
            uxp = ub[row, atp, cut].astype(F32)
            uxm = ub[row, atm, cut].astype(F32)
            uzp = up[row, at, cut].astype(F32)
            uzm = um[row, at, cut].astype(F32)
            if row == 0:
                uyp = ub[1, at, cut].astype(F32)
                uym = hal[0, at, cut].astype(F32) * first_ok
            else:
                uyp = hal[1, at, cut].astype(F32) * last_ok
                uym = ub[0, at, cut].astype(F32)
            for j in range(8):
                js = slice(j, j + 1)
                hyp = h_ref[4 + x, 1, js] if row == 0 else hyh[1, x, js]
                hym = hyh[0, x, js] if row == 0 else h_ref[x, 1, js]
                qq = h_ref[row * 4 + xm, 0, js] * uxm - h_ref[row * 4 + xp, 0, js] * uxp
                qq = qq + (hym * uym - hyp * uyp)
                qq = qq + (hzm[n, js] * uzm - hzp[n, js] * uzp)
                lines = pl.ds(g * 256 + j * 32, 32)
                q_ref[row, at, lines] = qq.astype(BF16)
            return carry

        return lax.fori_loop(0, 4, one, carry_in)

    def build_half(g):
        for row in range(2):
            lax.fori_loop(0, 3, functools.partial(build, g, row), 0)


    spans = [((0, 2), (2, 2)), ((0, 2), (2, 2)), ((0, 4),), ((0, 4),)]
    x_slot = e // 2 * 2 + z

    def x_copy(n, s, t):
        span = pl.ds(*spans[n][s])
        return rcopy(
            tb.at[n, span, e_ring[t]], xbuf.at[n, x_slot, span], x_s.at[n * 2 + s, t], x_r.at[n * 2 + s, x_slot],
            dev(zh * 8 + e_ring[t], vm),
        )

    def send_rows(n, s):
        start, count = spans[n][s]
        span = pl.ds(start, count)
        tb[n, span] = tf[n, pl.ds(start * 128, count * 128)].astype(BF16).reshape(count, 8, 16, 128)

        @pl.when(stays)
        def _():
            pltpu.make_async_copy(
                tb.at[n, span, e], xbuf.at[n, x_slot, span], x_r.at[n * 2 + s, x_slot]
            ).start()

        @pl.when(jnp.logical_not(stays))
        def _():
            x_copy(n, s, 0).start()

        for t in range(1, 8):
            x_copy(n, s, t).start()

    def products(first, s, parts):
        start, count = spans[first][s]
        total = None
        for r in range(2):
            pair = jnp.concatenate(
                [jnp.concatenate([ref[r, k] for k in range(12)], axis=1) for ref in parts], axis=0
            )
            left = jnp.concatenate(
                [q_ref[r, k, pl.ds(start * 128, count * 128)] for k in range(12)], axis=1
            )
            value = lax.dot_general(left, pair, NT, preferred_element_type=F32)
            total = value if total is None else total + value
        for k in range(len(parts) // 2):
            for g in range(count // 2):
                for j in range(8):
                    rows = slice(g * 256 + j * 32, g * 256 + j * 32 + 32)
                    tf[first + k, pl.ds(start * 128 + g * 256 + j, 32, stride=8), :] = total[
                        rows, k * 128 : (k + 1) * 128
                    ]
            send_rows(first + k, s)

    def z_copy(n, t):
        return rcopy(zsrc.at[n, lax.rem(zh + t, 4)], zbuf.at[n, t], z_s.at[n, t], z_r.at[n, t], dev(z_ring[t], m))

    def gather_batch(n):
        total = None
        for t in range(8):
            for s in range(len(spans[n])):
                landed = xbuf.at[n, t, pl.ds(*spans[n][s])]
                rcopy(landed, landed, x_s.at[n * 2 + s, t], x_r.at[n * 2 + s, t], here).wait_recv()
            value = xbuf[n, t].astype(F32)
            total = value if total is None else total + value
        zsrc[n] = total
        for t in range(1, 4):
            z_copy(n, t).start()

    for p in range(4):
        arrived(2, p)
    build_half(0)
    near = (ub, blk.at[2], blk.at[0], blk.at[1])
    products(0, 0, near)
    build_half(1)
    products(0, 1, near)
    for p in (0, 2, 1, 3):
        arrived(5, p)
        go(blk.at[5], 6, p, to_core)
    for p in range(4):
        arrived(3, p)
        arrived(4, p)
    products(2, 0, (blk.at[3], blk.at[4]))
    for p in range(4):
        arrived(6, p)
    products(3, 0, (blk.at[5], blk.at[6]))
    def pick_modes(k, carry):
        at = pl.ds(pl.multiple_of(k * 256, 256), 256)
        rows = lax.broadcasted_iota(jnp.int32, (512, 256), 0)
        onehot[:, at] = (rows == pmode_ref[:, at]).astype(F32).astype(BF16)
        return carry

    lax.fori_loop(0, 8, pick_modes, 0)
    mask[...] = (lax.broadcasted_iota(jnp.int32, (8, 2048), 0) == padv_ref[...]).astype(F32)

    amp_copy.wait()

    def split_amp(k, carry):
        at = pl.ds(pl.multiple_of(k * 32, 32), 32)
        value = amp[at]
        hi = value.astype(BF16)
        amp_hi[at] = hi
        amp_lo[at] = (value - hi.astype(F32)).astype(BF16)
        return carry

    lax.fori_loop(0, 64, split_amp, 0)

    for t in range(1, 8):
        rs_copy(t).wait_send()
        ag_copy(t, vm).wait_send()
    for t in range(8):
        hy_copy(t).wait_send()
    for copy in started + halo:
        copy.wait_send()
    take_token(2)
    for n in range(4):
        gather_batch(n)
    for n in range(4):
        for t in range(1, 8):
            for s in range(len(spans[n])):
                x_copy(n, s, t).wait_send()

    blocks = [
        (m, zb * 4 + y),
        (z * 4 + yprev, z * 4 + ynext),
        (zb * 4 + yprev, zb * 4 + ynext),
        (z * 4 + yfar, zb * 4 + yfar),
    ]
    for n in range(4):
        value = zsrc[n, zh]
        for t in range(1, 4):
            z_copy(n, t).wait_recv()
            value = value + zbuf[n, t]
        fin[blocks[n][0]] = value
        fin[blocks[n][1]] = pltpu.roll(value, 64, 1)

    low = lax.broadcasted_iota(jnp.int32, (16, 128), 1) < 64
    columns = []
    for t in range(4):
        columns.append(jnp.where(low, fin[2 * t], pltpu.roll(fin[2 * t + 1], 64, 1)))
    tensor = jnp.concatenate(columns, axis=1)
    out_ref[...] = tensor
    top = tensor.astype(BF16)
    rest = (tensor - top.astype(F32)).astype(BF16)
    chosen = jnp.dot(jnp.concatenate([top, rest], axis=0), onehot[...], preferred_element_type=F32)
    chosen = chosen[:16] + chosen[16:]
    first = jnp.sum(chosen[:8] * mask[...], axis=0, keepdims=True)
    second = jnp.sum(chosen[8:] * mask[...], axis=0, keepdims=True)
    rows = lax.broadcasted_iota(jnp.int32, (16, 2048), 0)
    both = jnp.where(lax.rem(rows, 2) == 0, first, second)
    both_hi = both.astype(BF16).astype(F32)
    stacked = jnp.where(rows < 2, both_hi, jnp.where(rows < 4, both - both_hi, 0.0)).astype(BF16)
    answer = jnp.dot(stacked, amp_hi[...], preferred_element_type=F32)
    answer = answer + jnp.dot(stacked, amp_lo[...], preferred_element_type=F32)
    resp_ref[...] = answer[0:2] + answer[2:4]

    for n in range(4):
        for t in range(1, 4):
            z_copy(n, t).wait_send()

    @pl.when(jnp.logical_not(stays))
    def _():
        rs_copy(0).wait_send()
        for p in range(4):
            swap(p).wait_send()
        for n in range(4):
            for s in range(len(spans[n])):
                x_copy(n, s, 0).wait_send()


def finish(tensor_ref, response_ref, out_ref, resp_ref):
    out_ref[...] = tensor_ref[...]
    resp_ref[...] = response_ref[...]


def shards(pod_modes, slab_map, slab_volume, advect_index, pair_adv, pair_mode, pair_amp):
    cells = pod_modes.shape[2] * pod_modes.shape[3] * lax.axis_size("cell") * pod_modes.shape[4]
    u = jnp.transpose(pod_modes, (3, 0, 2, 1, 4)).reshape(2, 12, 64, 128)
    vmem = pl.BlockSpec(memory_space=pltpu.VMEM)
    smem = pl.BlockSpec(memory_space=pltpu.SMEM)
    dma = pltpu.SemaphoreType.DMA
    shapes = (jax.ShapeDtypeStruct((16, 512), F32), jax.ShapeDtypeStruct((2, 1024), F32))
    results = pl.pallas_call(
        functools.partial(kernel, float(cells) ** -0.5),
        out_shape=shapes,
        in_specs=[vmem, vmem, smem, smem, vmem, vmem, pl.BlockSpec(memory_space=pl.ANY)],
        out_specs=(vmem, vmem),
        scratch_shapes=[
            pltpu.VMEM((2, 12, 64, 128), BF16),
            pltpu.VMEM((7, 2, 12, 64, 128), BF16),
            pltpu.VMEM((2, 12, 64, 128), BF16),
            pltpu.VMEM((2, 12, 64, 128), BF16),
            pltpu.VMEM((2, 12, 64, 128), BF16),
            pltpu.VMEM((2, 12, 512, 128), BF16),
            pltpu.VMEM((8, 3, 8, 128), F32),
            pltpu.VMEM((8, 3, 8, 128), F32),
            pltpu.VMEM((8, 3, 8, 128), F32),
            pltpu.VMEM((2, 4, 8, 128), F32),
            pltpu.VMEM((8, 8, 128), F32),
            pltpu.VMEM((8, 8, 128), F32),
            pltpu.VMEM((4, 512, 128), F32),
            pltpu.VMEM((4, 4, 8, 16, 128), BF16),
            pltpu.VMEM((4, 8, 4, 16, 128), BF16),
            pltpu.VMEM((4, 4, 16, 128), F32),
            pltpu.VMEM((4, 4, 16, 128), F32),
            pltpu.VMEM((8, 16, 128), F32),
            pltpu.VMEM((2048, 1024), F32),
            pltpu.VMEM((2048, 1024), BF16),
            pltpu.VMEM((2048, 1024), BF16),
            pltpu.VMEM((512, 2048), BF16),
            pltpu.VMEM((8, 2048), F32),
            dma((8,)), dma((8,)), dma((8,)), dma((8,)),
            dma((4,)), dma((4,)), dma((28,)), dma((28,)), dma((2,)), dma((2,)), dma((8,)), dma((8,)),
            dma((8, 8)), dma((8, 8)), dma((4, 4)), dma((4, 4)), dma,
            pltpu.SemaphoreType.REGULAR((3, 2)),
        ],
        compiler_params=pltpu.CompilerParams(
            collective_id=0, has_side_effects=True, vmem_limit_bytes=60 * 2**20
        ),
        name="pod_tensor",
    )(
        u, slab_map, slab_volume, advect_index,
        pair_adv.reshape(1, -1), pair_mode.reshape(1, -1), pair_amp,
    )
    tensor, response = pl.pallas_call(
        finish, out_shape=shapes, in_specs=[vmem, vmem], out_specs=(vmem, vmem), name="finish"
    )(*results)
    return tensor.reshape(2, 8, 512), response


def solution(mesh):
    in_specs = (P(None, "mode", None, "cell", None), P(None, "cell", None), P(), P(), P(), P(), P())
    out_specs = (P(("mode", "cell"), None, None), P(("mode", "cell"), None))
    return jax.shard_map(shards, mesh=mesh, in_specs=in_specs, out_specs=out_specs, check_vma=False)
```

```python
import functools
import jax
import jax.numpy as jnp
from jax import lax
from jax.experimental import pallas as pl
from jax.experimental.pallas import tpu as pltpu
from jax.sharding import PartitionSpec as P

MESH = pl.DeviceIdType.MESH
F32 = jnp.float32
BF16 = jnp.bfloat16
NT = (((1,), (1,)), ((), ()))


def kernel(
    scale,
    u_ref, slab_ref, vol_ref, adv_ref, padv_ref, pmode_ref, amp_hbm,
    out_ref, resp_ref,
    ub, blk, hal, up, um, q_ref,
    part, rs_buf, h_ref, hyh, hzp, hzm,
    tf, tb, xbuf, zsrc, zbuf, fin,
    amp, amp_hi, amp_lo, onehot, mask,
    rs_s, rs_r, ag_s, ag_r, own_s, own_r, bulk_s, bulk_r, halo_s, halo_r, hy_s, hy_r, x_s, x_r, z_s, z_r, amp_sem, token,
):
    q = lax.axis_index("cell")
    m = lax.axis_index("mode")
    core = lax.rem(q, 2)
    e = lax.rem(q, 8)
    zh = q // 8
    z = m // 4
    y = lax.rem(m, 4)
    zb = 1 - z
    stays = core == z
    vq = q - core + z
    vm = core * 4 + y
    ynext = lax.rem(y + 1, 4)
    yprev = lax.rem(y + 3, 4)
    yfar = lax.rem(y + 2, 4)

    def place(cell, block):
        return dev(cell - lax.rem(cell, 2) + block // 4, lax.rem(cell, 2) * 4 + lax.rem(block, 4))

    def dev(cell, mode):
        return {"cell": cell, "mode": mode}

    def rcopy(src, dst, send, recv, target):
        return pltpu.make_async_remote_copy(
            src_ref=src, dst_ref=dst, send_sem=send, recv_sem=recv,
            device_id=target, device_id_type=MESH,
        )

    here = dev(q, m)
    n_ring = [lax.rem(vm + t, 8) for t in range(8)]
    e_ring = [lax.rem(e + t, 8) for t in range(8)]
    z_ring = [lax.rem(zh + t, 4) * 8 + e for t in range(4)]
    vprev = lax.rem(vq + 31, 32)
    vnext = lax.rem(vq + 1, 32)
    qprev = lax.rem(q + 31, 32)
    qnext = lax.rem(q + 1, 32)

    barrier = pltpu.get_barrier_semaphore()
    z_up = dev(lax.rem(zh + z, 4) * 8 + e, zb * 4 + y)
    z_down = dev(lax.rem(zh + 3 + z, 4) * 8 + e, zb * 4 + y)
    y_of = [lax.rem(y + t, 4) for t in range(4)]
    peers = [place(vq, n_ring[t]) for t in range(1, 8)]
    peers += [dev(vq, lax.rem(z + t // 4, 2) * 4 + y_of[t % 4]) for t in range(1, 8)]
    peers += [
        dev(zh * 8 + lax.rem(e // 2 + t // 2, 4) * 2 + z, lax.rem(z + t, 2) * 4 + y) for t in range(1, 8)
    ]
    peers += [z_up, z_down]
    peers += [dev(vprev, vm), dev(vnext, vm)]
    peers += [place(vnext, x) for x in range(4)] + [place(vprev, 4 + x) for x in range(4)]

    def greet(peer, times):
        pl.semaphore_signal(barrier, inc=times, device_id=peer, device_id_type=MESH)

    for peer in peers:
        greet(peer, 1)

    @pl.when(jnp.logical_not(stays))
    def _():
        greet(dev(vq, m), 2)

    amp_copy = pltpu.make_async_copy(amp_hbm, amp, amp_sem)
    amp_copy.start()

    sub = lax.broadcasted_iota(jnp.int32, (8, 64), 0)
    wanted = jnp.zeros((8, 64), jnp.int32)
    for j in range(8):
        wanted = jnp.where(sub == j, adv_ref[j], wanted)
    owned = (wanted == m * 64 + lax.broadcasted_iota(jnp.int32, (8, 64), 1)).astype(F32).astype(BF16)
    for x in range(4):
        for row in range(2):
            ids = slab_ref[x, row : row + 1, :]
            vol = jnp.zeros((1, 128), F32)
            for level in range(8):
                vol = jnp.where(ids == level, vol_ref[level], vol)
            vol = vol * (0.5 * scale)
            for d in range(3):
                part[row * 4 + x, d] = vol * jnp.dot(owned, u_ref[row, d * 4 + x], preferred_element_type=F32)
    pl.semaphore_wait(barrier, jnp.where(stays, len(peers), len(peers) + 2))

    def piece(ref, p):
        return ref.at[p // 2, pl.ds((p % 2) * 6, 6)]

    def pass_token(k):
        pl.semaphore_signal(token.at[k, 0], inc=1, device_id=z_up, device_id_type=MESH)
        pl.semaphore_signal(token.at[k, 1], inc=1, device_id=z_down, device_id_type=MESH)

    def take_token(k):
        pl.semaphore_wait(token.at[k, 0], 1)
        pl.semaphore_wait(token.at[k, 1], 1)

    pass_token(0)

    def rs_copy(t):
        n = n_ring[t]
        return rcopy(part.at[n], rs_buf.at[m], rs_s.at[t], rs_r.at[m], place(core - z + vq, n))

    for t in range(1, 8):
        rs_copy(t).start()

    @pl.when(stays)
    def _():
        pltpu.make_async_copy(part.at[vm], rs_buf.at[m], rs_r.at[m]).start()
        for p in range(4):
            pltpu.make_async_copy(piece(u_ref, p), piece(ub, p), own_r.at[p]).start()

    def swap(p):
        return rcopy(piece(u_ref, p), piece(ub, p), own_s.at[p], own_r.at[p], dev(vq, vm))

    @pl.when(jnp.logical_not(stays))
    def _():
        rs_copy(0).start()
        for p in (0, 2, 1, 3):
            swap(p).start()

    up_y = place(vq, core * 4 + ynext)
    down_y = place(vq, core * 4 + yprev)
    to_core = place(vq, (1 - core) * 4 + y)

    def move(src, slot, p, target):
        return rcopy(piece(src, p), piece(blk.at[slot], p), bulk_s.at[slot * 4 + p], bulk_r.at[slot * 4 + p], target)

    started = []

    def go(src, slot, p, target):
        copy = move(src, slot, p, target)
        copy.start()
        started.append(copy)

    def arrived(slot, p):
        move(u_ref, slot, p, here).wait_recv()

    def start_first(p):
        swap(p).wait_recv()
        go(ub, 0, p, up_y)
        swap(p + 2).wait_recv()
        go(ub, 1, p + 2, down_y)

    def start_rest(p):
        go(ub, 0, p + 2, up_y)
        go(ub, 1, p, down_y)
        go(ub, 2, p, to_core)
        go(ub, 2, p + 2, to_core)

    halo = [
        rcopy(u_ref.at[0], hal.at[1], halo_s.at[0], halo_r.at[0], place(qprev, m)),
        rcopy(u_ref.at[1], hal.at[0], halo_s.at[1], halo_r.at[1], place(qnext, m)),
    ]
    for p in range(2):
        start_first(p)
    for p in range(2):
        start_rest(p)

    total = None
    for n in range(8):
        rcopy(part.at[n], rs_buf.at[n], rs_s.at[n], rs_r.at[n], here).wait_recv()
        total = rs_buf[n] if total is None else total + rs_buf[n]
    h_ref[vm] = total
    take_token(0)
    pass_token(1)

    def ag_copy(t, block):
        return rcopy(h_ref.at[block], h_ref.at[block], ag_s.at[t], ag_r.at[block], place(vq, n_ring[t]))

    vside = jnp.where(core == 0, vprev, vnext)

    def hy_copy(t):
        return rcopy(
            h_ref.at[vm, 1], hyh.at[1 - core, y], hy_s.at[t], hy_r.at[(1 - core) * 4 + y], place(vside, n_ring[t])
        )

    for t in range(8):
        if t > 0:
            ag_copy(t, vm).start()
        hy_copy(t).start()
    halo[0].start()
    halo[1].start()

    for p in range(2):
        arrived(0, p)
        go(blk.at[0], 5, p, up_y)
        go(blk.at[0], 3, p, to_core)
        arrived(1, p + 2)
        go(blk.at[1], 5, p + 2, down_y)
        go(blk.at[1], 4, p + 2, to_core)

    def shift(k, carry):
        for row in range(2):
            tile = ub[row, k].astype(F32)
            up[row, k] = pltpu.roll(tile, 127, 1).astype(BF16)
            um[row, k] = pltpu.roll(tile, 1, 1).astype(BF16)
        return carry

    lax.fori_loop(0, 12, shift, 0)

    for t in range(1, 8):
        ag_copy(t, n_ring[t]).wait_recv()
    take_token(1)
    pass_token(2)
    for n in range(8):
        hzp[n] = pltpu.roll(h_ref[n, 2], 127, 1)
        hzm[n] = pltpu.roll(h_ref[n, 2], 1, 1)

    for p in range(2):
        arrived(0, p + 2)
        go(blk.at[0], 3, p + 2, to_core)
        arrived(1, p)
        go(blk.at[1], 4, p, to_core)

    halo[0].wait_recv()
    halo[1].wait_recv()
    for i in range(2):
        for x in range(4):
            rcopy(hyh.at[i, x], hyh.at[i, x], hy_s.at[x], hy_r.at[i * 4 + x], here).wait_recv()

    first_ok = jnp.where(vq == 0, 0.0, 1.0)
    last_ok = jnp.where(vq == 31, 0.0, 1.0)

    def build(g, row, c, carry_in):
        def one(x, carry):
            xp = lax.rem(x + 1, 4)
            xm = lax.rem(x + 3, 4)
            at, atp, atm = c * 4 + x, c * 4 + xp, c * 4 + xm
            n = row * 4 + x
            cut = pl.ds(g * 32, 32)
            uxp = ub[row, atp, cut].astype(F32)
            uxm = ub[row, atm, cut].astype(F32)
            uzp = up[row, at, cut].astype(F32)
            uzm = um[row, at, cut].astype(F32)
            if row == 0:
                uyp = ub[1, at, cut].astype(F32)
                uym = hal[0, at, cut].astype(F32) * first_ok
            else:
                uyp = hal[1, at, cut].astype(F32) * last_ok
                uym = ub[0, at, cut].astype(F32)
            for j in range(8):
                js = slice(j, j + 1)
                hyp = h_ref[4 + x, 1, js] if row == 0 else hyh[1, x, js]
                hym = hyh[0, x, js] if row == 0 else h_ref[x, 1, js]
                qq = h_ref[row * 4 + xm, 0, js] * uxm - h_ref[row * 4 + xp, 0, js] * uxp
                qq = qq + (hym * uym - hyp * uyp)
                qq = qq + (hzm[n, js] * uzm - hzp[n, js] * uzp)
                lines = pl.ds(g * 256 + j * 32, 32)
                q_ref[row, at, lines] = qq.astype(BF16)
            return carry

        return lax.fori_loop(0, 4, one, carry_in)

    def build_half(g):
        for row in range(2):
            lax.fori_loop(0, 3, functools.partial(build, g, row), 0)


    spans = [((0, 2), (2, 2)), ((0, 2), (2, 2)), ((0, 4),), ((0, 4),)]
    x_slot = e // 2 * 2 + z

    def x_copy(n, s, t):
        span = pl.ds(*spans[n][s])
        return rcopy(
            tb.at[n, span, e_ring[t]], xbuf.at[n, x_slot, span], x_s.at[n * 2 + s, t], x_r.at[n * 2 + s, x_slot],
            dev(zh * 8 + e_ring[t], vm),
        )

    def send_rows(n, s):
        start, count = spans[n][s]
        span = pl.ds(start, count)
        tb[n, span] = tf[n, pl.ds(start * 128, count * 128)].astype(BF16).reshape(count, 8, 16, 128)

        @pl.when(stays)
        def _():
            pltpu.make_async_copy(
                tb.at[n, span, e], xbuf.at[n, x_slot, span], x_r.at[n * 2 + s, x_slot]
            ).start()

        @pl.when(jnp.logical_not(stays))
        def _():
            x_copy(n, s, 0).start()

        for t in range(1, 8):
            x_copy(n, s, t).start()

    def products(first, s, parts):
        start, count = spans[first][s]
        total = None
        for r in range(2):
            pair = jnp.concatenate(
                [jnp.concatenate([ref[r, k] for k in range(12)], axis=1) for ref in parts], axis=0
            )
            left = jnp.concatenate(
                [q_ref[r, k, pl.ds(start * 128, count * 128)] for k in range(12)], axis=1
            )
            value = lax.dot_general(left, pair, NT, preferred_element_type=F32)
            total = value if total is None else total + value
        for k in range(len(parts) // 2):
            for g in range(count // 2):
                for j in range(8):
                    rows = slice(g * 256 + j * 32, g * 256 + j * 32 + 32)
                    tf[first + k, pl.ds(start * 128 + g * 256 + j, 32, stride=8), :] = total[
                        rows, k * 128 : (k + 1) * 128
                    ]
            send_rows(first + k, s)

    def z_copy(n, t):
        return rcopy(zsrc.at[n, lax.rem(zh + t, 4)], zbuf.at[n, t], z_s.at[n, t], z_r.at[n, t], dev(z_ring[t], m))

    def gather_batch(n):
        total = None
        for t in range(8):
            for s in range(len(spans[n])):
                landed = xbuf.at[n, t, pl.ds(*spans[n][s])]
                rcopy(landed, landed, x_s.at[n * 2 + s, t], x_r.at[n * 2 + s, t], here).wait_recv()
            value = xbuf[n, t].astype(F32)
            total = value if total is None else total + value
        zsrc[n] = total
        for t in range(1, 4):
            z_copy(n, t).start()

    for p in range(4):
        arrived(2, p)
    build_half(0)
    near = (ub, blk.at[2], blk.at[0], blk.at[1])
    products(0, 0, near)
    for p in (0, 2, 1, 3):
        arrived(5, p)
        go(blk.at[5], 6, p, to_core)
    build_half(1)
    products(0, 1, near)
    for p in range(4):
        arrived(3, p)
        arrived(4, p)
    products(2, 0, (blk.at[3], blk.at[4]))
    for p in range(4):
        arrived(6, p)
    products(3, 0, (blk.at[5], blk.at[6]))
    def pick_modes(k, carry):
        at = pl.ds(pl.multiple_of(k * 256, 256), 256)
        rows = lax.broadcasted_iota(jnp.int32, (512, 256), 0)
        onehot[:, at] = (rows == pmode_ref[:, at]).astype(F32).astype(BF16)
        return carry

    lax.fori_loop(0, 8, pick_modes, 0)
    mask[...] = (lax.broadcasted_iota(jnp.int32, (8, 2048), 0) == padv_ref[...]).astype(F32)

    amp_copy.wait()

    def split_amp(k, carry):
        at = pl.ds(pl.multiple_of(k * 32, 32), 32)
        value = amp[at]
        hi = value.astype(BF16)
        amp_hi[at] = hi
        amp_lo[at] = (value - hi.astype(F32)).astype(BF16)
        return carry

    lax.fori_loop(0, 64, split_amp, 0)

    for t in range(1, 8):
        rs_copy(t).wait_send()
        ag_copy(t, vm).wait_send()
    for t in range(8):
        hy_copy(t).wait_send()
    for copy in started + halo:
        copy.wait_send()
    take_token(2)
    for n in range(4):
        gather_batch(n)
    for n in range(4):
        for t in range(1, 8):
            for s in range(len(spans[n])):
                x_copy(n, s, t).wait_send()

    blocks = [
        (m, zb * 4 + y),
        (z * 4 + yprev, z * 4 + ynext),
        (zb * 4 + yprev, zb * 4 + ynext),
        (z * 4 + yfar, zb * 4 + yfar),
    ]
    for n in range(4):
        value = zsrc[n, zh]
        for t in range(1, 4):
            z_copy(n, t).wait_recv()
            value = value + zbuf[n, t]
        fin[blocks[n][0]] = value
        fin[blocks[n][1]] = pltpu.roll(value, 64, 1)

    low = lax.broadcasted_iota(jnp.int32, (16, 128), 1) < 64
    columns = []
    for t in range(4):
        columns.append(jnp.where(low, fin[2 * t], pltpu.roll(fin[2 * t + 1], 64, 1)))
    tensor = jnp.concatenate(columns, axis=1)
    out_ref[...] = tensor
    top = tensor.astype(BF16)
    rest = (tensor - top.astype(F32)).astype(BF16)
    chosen = jnp.dot(jnp.concatenate([top, rest], axis=0), onehot[...], preferred_element_type=F32)
    chosen = chosen[:16] + chosen[16:]
    first = jnp.sum(chosen[:8] * mask[...], axis=0, keepdims=True)
    second = jnp.sum(chosen[8:] * mask[...], axis=0, keepdims=True)
    rows = lax.broadcasted_iota(jnp.int32, (16, 2048), 0)
    both = jnp.where(lax.rem(rows, 2) == 0, first, second)
    both_hi = both.astype(BF16).astype(F32)
    stacked = jnp.where(rows < 2, both_hi, jnp.where(rows < 4, both - both_hi, 0.0)).astype(BF16)
    answer = jnp.dot(stacked, amp_hi[...], preferred_element_type=F32)
    answer = answer + jnp.dot(stacked, amp_lo[...], preferred_element_type=F32)
    resp_ref[...] = answer[0:2] + answer[2:4]

    for n in range(4):
        for t in range(1, 4):
            z_copy(n, t).wait_send()

    @pl.when(jnp.logical_not(stays))
    def _():
        rs_copy(0).wait_send()
        for p in range(4):
            swap(p).wait_send()
        for n in range(4):
            for s in range(len(spans[n])):
                x_copy(n, s, 0).wait_send()


def finish(tensor_ref, response_ref, out_ref, resp_ref):
    out_ref[...] = tensor_ref[...]
    resp_ref[...] = response_ref[...]


def shards(pod_modes, slab_map, slab_volume, advect_index, pair_adv, pair_mode, pair_amp):
    cells = pod_modes.shape[2] * pod_modes.shape[3] * lax.axis_size("cell") * pod_modes.shape[4]
    u = jnp.transpose(pod_modes, (3, 0, 2, 1, 4)).reshape(2, 12, 64, 128)
    vmem = pl.BlockSpec(memory_space=pltpu.VMEM)
    smem = pl.BlockSpec(memory_space=pltpu.SMEM)
    dma = pltpu.SemaphoreType.DMA
    shapes = (jax.ShapeDtypeStruct((16, 512), F32), jax.ShapeDtypeStruct((2, 1024), F32))
    results = pl.pallas_call(
        functools.partial(kernel, float(cells) ** -0.5),
        out_shape=shapes,
        in_specs=[vmem, vmem, smem, smem, vmem, vmem, pl.BlockSpec(memory_space=pl.ANY)],
        out_specs=(vmem, vmem),
        scratch_shapes=[
            pltpu.VMEM((2, 12, 64, 128), BF16),
            pltpu.VMEM((7, 2, 12, 64, 128), BF16),
            pltpu.VMEM((2, 12, 64, 128), BF16),
            pltpu.VMEM((2, 12, 64, 128), BF16),
            pltpu.VMEM((2, 12, 64, 128), BF16),
            pltpu.VMEM((2, 12, 512, 128), BF16),
            pltpu.VMEM((8, 3, 8, 128), F32),
            pltpu.VMEM((8, 3, 8, 128), F32),
            pltpu.VMEM((8, 3, 8, 128), F32),
            pltpu.VMEM((2, 4, 8, 128), F32),
            pltpu.VMEM((8, 8, 128), F32),
            pltpu.VMEM((8, 8, 128), F32),
            pltpu.VMEM((4, 512, 128), F32),
            pltpu.VMEM((4, 4, 8, 16, 128), BF16),
            pltpu.VMEM((4, 8, 4, 16, 128), BF16),
            pltpu.VMEM((4, 4, 16, 128), F32),
            pltpu.VMEM((4, 4, 16, 128), F32),
            pltpu.VMEM((8, 16, 128), F32),
            pltpu.VMEM((2048, 1024), F32),
            pltpu.VMEM((2048, 1024), BF16),
            pltpu.VMEM((2048, 1024), BF16),
            pltpu.VMEM((512, 2048), BF16),
            pltpu.VMEM((8, 2048), F32),
            dma((8,)), dma((8,)), dma((8,)), dma((8,)),
            dma((4,)), dma((4,)), dma((28,)), dma((28,)), dma((2,)), dma((2,)), dma((8,)), dma((8,)),
            dma((8, 8)), dma((8, 8)), dma((4, 4)), dma((4, 4)), dma,
            pltpu.SemaphoreType.REGULAR((3, 2)),
        ],
        compiler_params=pltpu.CompilerParams(
            collective_id=0, has_side_effects=True, vmem_limit_bytes=60 * 2**20
        ),
        name="pod_tensor",
    )(
        u, slab_map, slab_volume, advect_index,
        pair_adv.reshape(1, -1), pair_mode.reshape(1, -1), pair_amp,
    )
    tensor, response = pl.pallas_call(
        finish, out_shape=shapes, in_specs=[vmem, vmem], out_specs=(vmem, vmem), name="finish"
    )(*results)
    return tensor.reshape(2, 8, 512), response


def solution(mesh):
    in_specs = (P(None, "mode", None, "cell", None), P(None, "cell", None), P(), P(), P(), P(), P())
    out_specs = (P(("mode", "cell"), None, None), P(("mode", "cell"), None))
    return jax.shard_map(shards, mesh=mesh, in_specs=in_specs, out_specs=out_specs, check_vma=False)
```
